32 devices in a mesh: layer: 4 (over x, core), latent: 8 (over z, y).
Axes of the slice: x: 2, y: 2, z: 4, core: 2. Of those that a mesh axis runs over, the one named last changes fastest.
Arguments:
- acts: bfloat16 [4, 512, 2048], P('layer', None, 'latent'), may hold values from -6 to 6
- w_enc: bfloat16 [4, 2048, 4096], P('layer', None, 'latent'), may hold values from -0.0625 to 0.0625
- b_enc: float32 [4096], P('latent'), may hold values from -3 to 3
- w_dec: bfloat16 [4, 4096, 2048], P('layer', 'latent'), may hold values from -0.125 to 0.125
- b_dec: bfloat16 [4, 2048], P('layer', 'latent'), may hold values from -3 to 3
Outputs:
- grad_enc: bfloat16 [4, 2048, 4096], P('layer', None, 'latent')
- grad_dec: bfloat16 [4, 4096, 2048], P('layer', 'latent')
- grad_benc: float32 [4096], P('latent')
- grad_bdec: float32 [4, 2048], P('layer', 'latent')
The draws below stay inside these ranges and needn't reach their ends.
All inputs are finite; a program needn't handle non-finite values.
Results may differ from the reference program's by a relative error of at most 0.014.
Values may be sent and summed in bfloat16 or wider, within the bound.
A program may use at most 64 MiB of HBM per device.

```python
import jax
import jax.numpy as jnp

D = 4096
LAYERS = 2
TOK = 512
LATENTS = 4096


def with_spikes(entries, rng, source, target, shards_of, factor):
    def block_of(position):
        return (jnp.arange(entries.shape[position]) // (entries.shape[position] // shards_of)).reshape((-1,) + (1,) * (entries.ndim - 1 - position))

    near = jax.random.permutation(rng, shards_of)[block_of(target)]
    second = (block_of(target) + shards_of // 2) % shards_of
    return jnp.where((block_of(source) == near) | (block_of(source) == second), factor * entries, entries)


def levels(key, dims, shards, low, top_value):
    factor_of, own = 1.0, jax.random.fold_in(key, 6)
    for axis_at, blocks in shards:
        heights = jnp.exp(jax.random.uniform(jax.random.fold_in(own, axis_at), (blocks,), jnp.float32, low / len(shards), top_value / len(shards)))
        factor_of = factor_of * jnp.repeat(heights, dims[axis_at] // blocks).reshape([-1 if axis == axis_at else 1 for axis in range(len(dims))])
    return factor_of


def centred(stream_key, shape, width, reach, shards=(), kind=jnp.bfloat16):
    result = jax.random.normal(stream_key, shape, jnp.float32) * width
    if len(shards) > 0:
        result = levels(stream_key, shape, shards, -0.22, 0.18) * result
    return jnp.clip(result, min=-reach, max=reach).astype(kind)


def bell_draw_with(stream_key, extent, deviation, bound, split, heavy, kind=jnp.bfloat16):
    entries = deviation * jax.random.normal(stream_key, extent, jnp.float32)
    if split:
        entries = entries * levels(stream_key, extent, split, -0.22, 0.18)
    return jnp.clip(with_spikes(entries, jax.random.fold_in(stream_key, 3), *heavy), -bound, bound).astype(kind)


def setup_inputs(seed: int = 0) -> dict:
    seeds = jax.random.split(jax.random.key(seed), 6)
    return {
        "acts": centred(seeds[0], (2 * LAYERS, TOK, D // 2), 1.0, 6.0, ((0, 4), (2, 8))),
        "w_enc": centred(seeds[1], (2 * LAYERS, D // 2, LATENTS), (LAYERS * D) ** -0.5, 0.0625, ((0, 4), (2, 8))),
        "b_enc": centred(seeds[2], (LATENTS,), 0.5, 3.0, ((0, 8),), jnp.float32),
        "w_dec": bell_draw_with(seeds[3], (2 * LAYERS, LATENTS, D // 2), LATENTS ** -0.5, 0.125, ((0, 4), (1, 8)), (1, 2, 8, 2.0)),
        "b_dec": centred(seeds[4], (2 * LAYERS, D // 2), 0.5, 3.0, ((0, 4), (1, 8))),
    }


def reference(acts, w_enc, b_enc, w_dec, b_dec):
    half = D // 2
    full_acts = [jnp.concatenate([acts[2 * i], acts[2 * i + 1]], axis=1) for i in range(LAYERS)]
    full_enc = [jnp.concatenate([w_enc[2 * i], w_enc[2 * i + 1]], axis=0) for i in range(LAYERS)]
    full_dec = [jnp.concatenate([w_dec[2 * i], w_dec[2 * i + 1]], axis=1) for i in range(LAYERS)]
    full_bias = [jnp.concatenate([b_dec[2 * i], b_dec[2 * i + 1]], axis=0) for i in range(LAYERS)]
    pre = jnp.zeros((TOK, LATENTS), jnp.float32) + b_enc[None, :].astype(jnp.float32)
    for layer_idx in range(LAYERS):
        pre = pre + jnp.dot(full_acts[layer_idx], full_enc[layer_idx], preferred_element_type=jnp.float32)
    feat = (jax.nn.softplus(4.0 * pre) / 4.0).astype(jnp.bfloat16)
    scale = TOK ** -0.5
    grad_feat = jnp.zeros((TOK, LATENTS), jnp.float32)
    dec_list = []
    bdec_list = []
    for layer_idx in range(LAYERS):
        recon = jnp.dot(feat, full_dec[layer_idx], preferred_element_type=jnp.float32)
        err = (recon + full_bias[layer_idx][None, :].astype(jnp.float32) - full_acts[layer_idx].astype(jnp.float32)).astype(jnp.bfloat16)
        bias_grad = scale * jnp.sum(err.astype(jnp.float32), axis=0)
        bdec_list.append(bias_grad[:half])
        bdec_list.append(bias_grad[half:])
        dec_grad = (scale * jnp.dot(feat.T, err, preferred_element_type=jnp.float32)).astype(jnp.bfloat16)
        dec_list.append(dec_grad[:, :half])
        dec_list.append(dec_grad[:, half:])
        grad_feat = grad_feat + jnp.dot(err, full_dec[layer_idx].T, preferred_element_type=jnp.float32)
    grad_feat = scale * grad_feat
    grad_pre = grad_feat * jax.nn.sigmoid(4.0 * pre)
    grad_benc = jnp.sum(grad_pre, axis=0)
    grad_pre_b = grad_pre.astype(jnp.bfloat16)
    enc_list = []
    for layer_idx in range(LAYERS):
        enc_grad = jnp.dot(full_acts[layer_idx].T, grad_pre_b, preferred_element_type=jnp.float32).astype(jnp.bfloat16)
        enc_list.append(enc_grad[:half])
        enc_list.append(enc_grad[half:])
    return jnp.stack(enc_list), jnp.stack(dec_list), grad_benc, jnp.stack(bdec_list)
```

```python
import functools

import jax
import jax.numpy as jnp
from jax import lax
from jax.experimental import pallas as pl
from jax.experimental.pallas import tpu as pltpu
from jax.sharding import PartitionSpec as P

MESH = pl.DeviceIdType.MESH
F32 = jnp.float32
BF16 = jnp.bfloat16
INNER = 2
VMEM_LIMIT = 60 * 1024 * 1024
SHARES = (2, 2, 2, 1, 1)
PLAN = dict(
    direct=(0, 3), act=(0.0, 4.0, 9.0, 13.0, 16.0), act_hop=3.0, use=0.3, gap=(3.0, 3.0),
    out=(16.0, 21.0, 27.0, 33.0, 36.0), out_hop=3.0, near=3.0, err=(0.0,) * 5, err_hop=3.0,
)
SINGLE = dict(
    direct=(), act=(0.0,), act_hop=3.0, use=0.3, gap=(3.0, 3.0),
    out=(0.0,), out_hop=3.0, near=3.0, err=(0.0,), err_hop=3.0,
)


def remote(src, dst, send, recv, axis, index):
    return pltpu.make_async_remote_copy(
        src_ref=src,
        dst_ref=dst,
        send_sem=send,
        recv_sem=recv,
        device_id={axis: index},
        device_id_type=MESH,
    )


def dot(a, b, dims=((1,), (0,))):
    return lax.dot_general(a, b, (dims, ((), ())), preferred_element_type=F32)


def step_kernel(n, sizes, plan, flat, scale, acts_hbm, enc_hbm, dec_hbm, benc_hbm, bdec_hbm, *refs):
    if flat:
        (genc, gdec, gbenc, gbdec), refs = refs[:4], refs[4:]
        (full, err, feat, gpre, turned, feat_turned), refs = refs[:6], refs[6:]
    else:
        (full, err, feat, gpre, gbenc, gbdec), refs = refs[:6], refs[6:]
    (
        enc, dec, benc_ref, bdec_ref, part, own,
        side_out, side_in, line_out, line_in,
        xup_out, xup_in, xdown_out, xdown_in, sum_out, sum_in, total, gate,
        load_sem, ag_send, ag_recv, eg_send, eg_recv,
        side_sem, up_sem, down_sem, xup_sem, xdown_sem, sum_sem,
    ) = refs
    depth = n // INNER
    tokens, width = acts_hbm.shape
    chunks = len(sizes)
    me = lax.axis_index("latent")
    z, y = me // INNER, lax.rem(me, INNER)
    partner = z * INNER + 1 - y
    layer = lax.axis_index("layer")
    peers = 4
    not_top, not_bottom = z < depth - 1, z > 0

    barrier = pltpu.get_barrier_semaphore()

    def greet(axis, index):
        pl.semaphore_signal(barrier, inc=1, device_id={axis: index}, device_id_type=MESH)

    greet("latent", partner)
    pl.when(not_top)(lambda: greet("latent", me + INNER))
    pl.when(not_bottom)(lambda: greet("latent", me - INNER))
    for k in range(1, peers):
        greet("layer", lax.rem(layer + k, peers))
    loads = [
        pltpu.make_async_copy(acts_hbm, full.at[me], load_sem.at[0]),
        pltpu.make_async_copy(benc_hbm, benc_ref, load_sem.at[1]),
        pltpu.make_async_copy(bdec_hbm, bdec_ref, load_sem.at[2]),
        pltpu.make_async_copy(enc_hbm, enc, load_sem.at[3]),
        pltpu.make_async_copy(dec_hbm, dec, load_sem.at[4]),
    ]
    for load in loads:
        load.start()
    pl.semaphore_wait(
        barrier, peers + jnp.where(not_top, 1, 0) + jnp.where(not_bottom, 1, 0)
    )

    gbdec[...] = jnp.zeros_like(gbdec)
    gbenc[...] = jnp.zeros_like(gbenc)

    starts = [sum(sizes[:c]) for c in range(chunks)]

    def span(c):
        return pl.ds(starts[c], sizes[c])

    def direct(c):
        return c in plan["direct"]

    def share(c, peer):
        quarter = sizes[c] // peers
        return pl.ds(pl.multiple_of(starts[c] + peer * quarter, quarter), quarter)

    def slot(c):
        return pl.ds(starts[c] // peers, sizes[c] // peers)

    def enc_rows(b):
        return enc[pl.ds(pl.multiple_of(b * width, width), width), :]

    def dec_columns(b):
        if flat:
            return dec[:, pl.ds(pl.multiple_of(b * width, width), width)]
        return dec[b]

    targets = (partner, me + INNER, me - INNER)

    def gather_copy(buf, send, recv, c, b, way, source=None):
        spot = buf.at[b, span(c), :]
        return remote(
            spot if source is None else source, spot,
            send.at[c, b, way], recv.at[c, b], "latent", targets[way],
        )

    def gather_own(buf, send, recv, c, source, act):
        def go(way):
            act(gather_copy(buf, send, recv, c, me, way, source))

        pl.when(not_top)(lambda: go(1))
        pl.when(not_bottom)(lambda: go(2))
        go(0)

    def gather_line(buf, send, recv, c, d, below, act, wait):
        at = z - d if below else z + d

        @pl.when(at >= 0 if below else at < depth)
        def _():
            b = at * INNER + y
            if wait:
                gather_copy(buf, send, recv, c, b, 0).wait_recv()
            way = 1 if below else 2

            @pl.when(not_top if below else not_bottom)
            def _():
                act(gather_copy(buf, send, recv, c, b, way))

            if not (direct(c) and d == 1):
                act(gather_copy(buf, send, recv, c, b, 0))

    def gather_side(buf, send, recv, c, d, below, act, wait):
        at = z - d if below else z + d

        @pl.when(at >= 0 if below else at < depth)
        def _():
            b = at * INNER + 1 - y
            if wait:
                gather_copy(buf, send, recv, c, b, 0).wait_recv()
            if direct(c) and d == 0:
                for way, valid in ((1, not_top), (2, not_bottom)):

                    @pl.when(valid)
                    def _():
                        act(gather_copy(buf, send, recv, c, b, way))

    def on_block(d, below, side, use):
        at = z - d if below else z + d

        @pl.when(at >= 0 if below else at < depth)
        def _():
            use(at * INNER + (1 - y if side else y))

    def start(copy):
        copy.start()

    def finish(copy):
        copy.wait_send()

    events = []

    def event(time, function, *args):
        events.append((time, len(events), functools.partial(function, *args)))

    def gather_events(buf, send, recv, c, source, time, hop, use):
        event(time, gather_own, buf, send, recv, c, source, start)
        event(time + 0.1, use, c, me)
        for d in range(1, depth):
            for below in (True, False):
                at = time + d * hop
                event(at, gather_line, buf, send, recv, c, d, below, start, True)
                event(at + plan["use"], on_block, d, below, False, functools.partial(use, c))
        for d in range(depth):
            for below in (True, False) if d else (True,):
                at = time + (d + 1) * hop + 0.2
                event(at, gather_side, buf, send, recv, c, d, below, start, True)
                event(at + 0.3, on_block, d, below, True, functools.partial(use, c))
        return time + depth * hop + 0.6

    def gather_finish(buf, send, recv, c, source):
        gather_own(buf, send, recv, c, source, finish)
        for d in range(1, depth):
            for below in (True, False):
                gather_line(buf, send, recv, c, d, below, finish, False)
        gather_side(buf, send, recv, c, 0, True, finish, False)

    def sum_copy(s, c, phase, k):
        peer = lax.rem(layer + k, peers)
        if phase == 0:
            src = sum_out.at[s, share(c, peer), :]
            dst = sum_in.at[s, k - 1, slot(c), :]
        else:
            src = total.at[s, share(c, layer), :]
            dst = src
        return remote(
            src, dst, sum_sem.at[s, c, phase, 0, k - 1], sum_sem.at[s, c, phase, 1, k - 1],
            "layer", peer,
        )

    def sum_first(s, c):
        sum_out[s, span(c), :] = part[s, span(c), :].astype(BF16)
        for k in (2, 1, 3):
            sum_copy(s, c, 0, k).start()

    def sum_second(s, c):
        for k in range(1, peers):
            sum_copy(s, c, 0, k).wait_recv()
        mine = share(c, layer)
        value = part[s, mine, :]
        for k in range(1, peers):
            value = value + sum_in[s, k - 1, slot(c), :].astype(F32)
        total[s, mine, :] = value.astype(BF16)
        for k in (2, 1, 3):
            sum_copy(s, c, 1, k).start()

    def sum_third(s, c):
        for k in range(1, peers):
            sum_copy(s, c, 1, k).wait_recv()

    def sum_finish(s, c):
        for k in range(1, peers):
            sum_copy(s, c, 0, k).wait_send()
            sum_copy(s, c, 1, k).wait_send()

    def use_act(c, b):
        value = dot(full[b, span(c), :], enc_rows(b))
        part[0, span(c), :] = value if b is me else part[0, span(c), :] + value

    def use_err(c, b):
        value = dot(err[b, span(c), :], dec_columns(b), ((1,), (1,)))
        part[1, span(c), :] = value if b is me else part[1, span(c), :] + value

    def activate(c):
        sum_third(0, c)
        wide = 4.0 * (total[0, span(c), :].astype(F32) + benc_ref[...])
        soft = jnp.maximum(wide, 0.0) + jnp.log1p(jnp.exp(-jnp.abs(wide)))
        feat[span(c), :] = (soft * 0.25).astype(BF16)

    def open_gate(c):
        wide = 4.0 * (total[0, span(c), :].astype(F32) + benc_ref[...])
        gate[span(c), :] = scale * jax.nn.sigmoid(wide)

    def term(c, b):
        return dot(feat[span(c), :], dec_columns(b))

    def side_copy(c, at):
        return remote(
            side_out.at[at, span(c), :], side_in.at[at, span(c), :],
            side_sem.at[0, c, at], side_sem.at[1, c, at], "latent", partner,
        )

    def land(at, up):
        return at + 1 if up else at

    def line_copy(c, at, up):
        sems = up_sem if up else down_sem
        return remote(
            line_out.at[at, span(c), :], line_in.at[land(at, up), span(c), :], sems.at[0, c, at], sems.at[1, c, at],
            "latent", me + INNER if up else me - INNER,
        )

    def cross_copy(c, up):
        out, land, sems = (xup_out, xup_in, xup_sem) if up else (xdown_out, xdown_in, xdown_sem)
        return remote(
            out.at[span(c), :], land.at[span(c), :], sems.at[0, c], sems.at[1, c],
            "latent", me + INNER if up else me - INNER,
        )

    def at_distance(d, up, use):
        at = z + d if up else z - d
        pl.when(at < depth if up else at >= 0)(lambda: use(at))

    def scatter_other(c, d, up):
        def go(at):
            value = term(c, at * INNER + 1 - y).astype(BF16)
            if direct(c) and d == 1:
                out = xup_out if up else xdown_out
                out[span(c), :] = value
                cross_copy(c, up).start()
            else:
                side_out[at, span(c), :] = value
                side_copy(c, at).start()

        at_distance(d, up, go)

    def scatter_other_near(c):
        value = term(c, z * INNER + 1 - y)
        if not direct(c):
            side_out[z, span(c), :] = value.astype(BF16)
            side_copy(c, z).start()
            return
        own[z, span(c), :] = value
        for up, valid in ((True, not_bottom), (False, not_top)):

            @pl.when(valid)
            def _():
                cross_copy(c, up).wait_recv()
                own[z, span(c), :] = own[z, span(c), :] + (xup_in if up else xdown_in)[span(c), :].astype(F32)

        side_out[z, span(c), :] = own[z, span(c), :].astype(BF16)
        side_copy(c, z).start()

    def scatter_own(c, d, up):
        def go(at):
            own[at, span(c), :] = term(c, at * INNER + y)

        at_distance(d, up, go)

    def scatter_line(c, d, up):
        inner = not_bottom if up else not_top

        def go(at):
            value = own[at, span(c), :]
            if not (direct(c) and d == 1):
                side_copy(c, at).wait_recv()
                value = value + side_in[at, span(c), :].astype(F32)

            @pl.when(inner)
            def _():
                line_copy(c, at, up).wait_recv()
                line_out[at, span(c), :] = (
                    value + line_in[land(at, up), span(c), :].astype(F32)
                ).astype(BF16)

            @pl.when(jnp.logical_not(inner))
            def _():
                line_out[at, span(c), :] = value.astype(BF16)

            line_copy(c, at, up).start()

        at_distance(d, up, go)

    def scatter_last(c):
        side_copy(c, z).wait_recv()
        value = own[z, span(c), :] + side_in[z, span(c), :].astype(F32)
        own[z, span(c), :] = value + bdec_ref[...].astype(F32) - full[me, span(c), :].astype(F32)
        for up, valid in ((True, not_bottom), (False, not_top)):

            @pl.when(valid)
            def _():
                line_copy(c, z, up).wait_recv()
                own[z, span(c), :] = own[z, span(c), :] + line_in[land(z, up), span(c), :].astype(F32)

        value = own[z, span(c), :].astype(BF16)
        err[me, span(c), :] = value
        gbdec[...] = gbdec[...] + scale * jnp.sum(value.astype(F32), axis=0, keepdims=True)

    def scatter_finish(c):
        for d in range(depth - 1, 0, -1):
            for up in (True, False):
                if direct(c) and d == 1:
                    at_distance(d, up, lambda at: cross_copy(c, up).wait_send())
                else:
                    at_distance(d, up, lambda at: side_copy(c, at).wait_send())
                at_distance(d, up, lambda at: line_copy(c, at, up).wait_send())
        side_copy(c, z).wait_send()

    def close(c):
        sum_third(1, c)
        value = total[1, span(c), :].astype(F32) * gate[span(c), :]
        gbenc[...] = gbenc[...] + jnp.sum(value, axis=0, keepdims=True)
        gpre[span(c), :] = value.astype(BF16)

    def own_near(c):
        own[z, span(c), :] = term(c, z * INNER + y)

    def turn(b):
        turned[pl.ds(b * width, width), :] = full[b].T

    def turn_feat():
        feat_turned[...] = feat[...].T

    def finish_dec(b):
        columns = pl.ds(b * width, width)
        gdec[:, columns] = (scale * dot(feat_turned[...], err[b])).astype(BF16)

    def finish_enc(b):
        lines = pl.ds(b * width, width)
        genc[lines, :] = dot(turned[lines, :], gpre[...]).astype(BF16)

    source = lambda c: acts_hbm.at[span(c), :]
    event(0.05, loads[0].wait)
    event(0.06, loads[3].wait)
    event(2.0, loads[1].wait)
    event(2.0, loads[2].wait)
    event(2.0, loads[4].wait)
    last = closing = 0.0
    gap = plan["gap"]
    for c in range(chunks):
        ready = gather_events(
            full, ag_send, ag_recv, c, source(c), plan["act"][c], plan["act_hop"], use_act
        )
        last = max(last, ready)
        event(ready, sum_first, 0, c)
        event(ready + gap[0], sum_second, 0, c)
        event(ready + gap[0] + gap[1], activate, c)
        begin = max(ready + gap[0] + gap[1] + 0.05, plan["out"][c])
        hop = plan["out_hop"]
        for d in range(depth - 1, 0, -1):
            for up in (True, False):
                event(begin, scatter_other, c, d, up)
        for d in range(depth - 1, 0, -1):
            for up in (True, False):
                event(begin + 0.2, scatter_own, c, d, up)
                event(begin + 0.5 + (depth - d) * hop, scatter_line, c, d, up)
        event(begin + (plan["near"] if direct(c) else 0.3), scatter_other_near, c)
        own_time = max(begin + hop, begin + plan["near"]) + 0.1
        event(own_time, own_near, c)
        event(own_time + 0.1, open_gate, c)
        done = max(begin + 0.6 + depth * hop, own_time + 0.2)
        event(done, scatter_last, c)
        begin = max(done + 0.05, plan["err"][c])
        ready = gather_events(
            err, eg_send, eg_recv, c, None, begin, plan["err_hop"], use_err
        )
        event(ready, sum_first, 1, c)
        event(ready + gap[0], sum_second, 1, c)
        event(ready + gap[0] + gap[1], close, c)
        closing = max(closing, ready)
    if flat:
        for b in range(n):
            event(last + 2.0 + b, turn, b)
            event(closing + (0.01 if b < n // 2 else gap[0] + 0.01), finish_dec, b)
            event(closing + gap[0] + gap[1] + 1.0, finish_enc, b)
        event(closing - 1.0, turn_feat)
    for _, _, function in sorted(events, key=lambda e: e[:2]):
        function()
    for c in range(chunks):
        gather_finish(full, ag_send, ag_recv, c, source(c))
        gather_finish(err, eg_send, eg_recv, c, None)
        scatter_finish(c)
        for s in range(2):
            sum_finish(s, c)


def body(n, acts, w_enc, b_enc, w_dec, b_dec):
    local, enc, dec = acts[0], w_enc[0], w_dec[0]
    tokens, width = local.shape
    latents = enc.shape[1]
    depth = n // INNER
    flat = width % 128 == 0 and latents % 128 == 0
    unit = tokens // sum(SHARES)
    if flat and tokens % sum(SHARES) == 0 and unit % 64 == 0:
        sizes, plan = [unit * s for s in SHARES], PLAN
    else:
        sizes, plan = [tokens], SINGLE
    chunks = len(sizes)
    scale = tokens ** (-0.5)
    if not flat:
        dec = dec.reshape(latents, n, width).transpose(1, 0, 2)
    vmem = pl.BlockSpec(memory_space=pltpu.VMEM)
    hbm = pl.BlockSpec(memory_space=pl.ANY)
    dma = pltpu.SemaphoreType.DMA
    blocks = (n, tokens, width)
    hidden = (tokens, latents)
    side = pltpu.VMEM((depth, tokens, width), BF16)
    line = pltpu.VMEM((depth + 1, tokens, width), BF16)
    cross = pltpu.VMEM((tokens, width), BF16)
    small = (jax.ShapeDtypeStruct((1, latents), F32), jax.ShapeDtypeStruct((1, width), F32))
    inner = (blocks, blocks, hidden, hidden)
    if flat:
        outs = (pltpu.VMEM((n * width, latents), BF16), pltpu.VMEM((latents, n * width), BF16))
        extra = [pltpu.VMEM(shape, BF16) for shape in inner]
        extra += [pltpu.VMEM((n * width, tokens), BF16), pltpu.VMEM((latents, tokens), BF16)]
    else:
        outs = tuple(jax.ShapeDtypeStruct(shape, BF16) for shape in inner)
        extra = []
    results = pl.pallas_call(
        functools.partial(step_kernel, n, sizes, plan, flat, scale),
        out_shape=outs + small,
        in_specs=[hbm] * 5,
        out_specs=(vmem,) * (len(outs) + 2),
        scratch_shapes=extra + [
            pltpu.VMEM(enc.shape, BF16),
            pltpu.VMEM(dec.shape, BF16),
            pltpu.VMEM((1, latents), F32),
            pltpu.VMEM((1, width), BF16),
            pltpu.VMEM((2,) + hidden, F32),
            pltpu.VMEM((depth, tokens, width), F32),
            side, side, line, line,
            cross, cross, cross, cross,
            pltpu.VMEM((2,) + hidden, BF16),
            pltpu.VMEM((2, 3, tokens // 4, latents), BF16),
            pltpu.VMEM((2,) + hidden, BF16),
            pltpu.VMEM(hidden, F32),
            dma((5,)),
            dma((chunks, n, 3)),
            dma((chunks, n)),
            dma((chunks, n, 3)),
            dma((chunks, n)),
            dma((2, chunks, depth)),
            dma((2, chunks, depth)),
            dma((2, chunks, depth)),
            dma((2, chunks)),
            dma((2, chunks)),
            dma((2, chunks, 2, 2, 3)),
        ],
        compiler_params=pltpu.CompilerParams(
            collective_id=0, has_side_effects=True,
            vmem_limit_bytes=VMEM_LIMIT - (4 * n * width * latents if flat else 0),
        ),
        name="step",
    )(local, enc, dec, b_enc[None, :], b_dec)
    gbenc, gbdec = results[-2:]
    if flat:
        genc, gdec = results[:2]
    else:
        full, err, feat, gpre = results[:4]
        genc = jnp.einsum("btw,tl->bwl", full, gpre, preferred_element_type=F32)
        genc = genc.astype(BF16).reshape(n * width, latents)
        gdec = jnp.einsum("tl,btw->lbw", feat, err, preferred_element_type=F32)
        gdec = (scale * gdec).astype(BF16).reshape(latents, n * width)
    return genc[None], gdec[None], gbenc[0], gbdec


def solution(mesh):
    return jax.shard_map(
        functools.partial(body, mesh.shape["latent"]),
        mesh=mesh,
        in_specs=(
            P("layer", None, "latent"),
            P("layer", None, "latent"),
            P("latent"),
            P("layer", "latent", None),
            P("layer", "latent"),
        ),
        out_specs=(
            P("layer", None, "latent"),
            P("layer", "latent", None),
            P("latent"),
            P("layer", "latent"),
        ),
        check_vma=False,
    )
```

```python
import functools

import jax
import jax.numpy as jnp
from jax import lax
from jax.experimental import pallas as pl
from jax.experimental.pallas import tpu as pltpu
from jax.sharding import PartitionSpec as P

MESH = pl.DeviceIdType.MESH
F32 = jnp.float32
BF16 = jnp.bfloat16
INNER = 2
VMEM_LIMIT = 60 * 1024 * 1024
SHARES = (1, 1, 1, 1)
PLAN = {'use': 1.03,
 'chunks': [{'act': (0, [0.0, 1.0, 1.8], [5.9, 3.3, 6.0, 4.8]),
             'sums': (9.4, 10.3),
             'out': 6.9,
             'line': [3.4, 36.6, 40.6],
             'near': 30.8,
             'own': 53.6,
             'done': 4.0,
             'err': (26.9, [60.7, 68.1, 79.3], [90.0, 87.1, 110.9, 102.0]),
             'last_sums': (16.7, 28.3),
             'cross': (False, True, False),
             'chain': (3, 1, 3)},
            {'act': (0, [0.9, 1.4, 2.6], [0.0, 7.4, 9.9, 8.6]),
             'sums': (8.8, 10.0),
             'out': 42.5,
             'line': [58.3, 47.9, 34.1],
             'near': 13.2,
             'own': 8.6,
             'done': 66.5,
             'err': (10.6, [83.9, 98.4, 82.9], [96.5, 126.6, 125.6, 107.4]),
             'last_sums': (23.3, 87.6),
             'cross': (False, False, False),
             'chain': (3, 1, 2)},
            {'act': (0.1, [1.7, 10.1, 12.4], [21.6, 29.3, 26.5, 25.6]),
             'sums': (15.1, 14.9),
             'out': 50.9,
             'line': [0.5, 2.6, 27.9],
             'near': 41.5,
             'own': 73.2,
             'done': 39.1,
             'err': (12.0, [112.8, 131.1, 102.9], [135.0, 132.8, 188.2, 128.9]),
             'last_sums': (38.2, 7.0),
             'cross': (True, False, False),
             'chain': (3, 1, 2)},
            {'act': (2.7, [11.1, 25.0, 18.6], [18.6, 42.2, 49.5, 36.5]),
             'sums': (10.2, 7.1),
             'out': 65.6,
             'line': [87.7, 10.4, 68.0],
             'near': 24.8,
             'own': 87.4,
             'done': 115.6,
             'err': (101.3, [159.3, 148.8, 140.7], [145.7, 194.6, 202.3, 191.1]),
             'last_sums': (25.1, 64.5),
             'cross': (True, False, True),
             'chain': (2, 2, 1)}]}


def default_plan(depth, chunks):
    plan = []
    for c in range(chunks):
        begin, hop = 4.0 * c, 3.0
        act = begin, [begin + d * hop for d in range(1, depth)], [begin + (d + 1) * hop for d in range(depth)]
        out = begin + (depth + 3) * hop
        done = out + (depth + 1) * hop
        err = done, [done + d * hop for d in range(1, depth)], [done + (d + 1) * hop for d in range(depth)]
        plan.append(dict(
            act=act, sums=(hop, hop), out=out, line=[out + (depth - d) * hop for d in range(1, depth)],
            near=out + 0.3, own=out + hop, done=done, err=err, last_sums=(hop, hop),
            cross=(False, False, False), chain=(depth - 1,) * 3,
        ))
    return dict(use=0.3, chunks=plan)


def remote(src, dst, send, recv, axis, index):
    return pltpu.make_async_remote_copy(
        src_ref=src,
        dst_ref=dst,
        send_sem=send,
        recv_sem=recv,
        device_id={axis: index},
        device_id_type=MESH,
    )


def dot(a, b, dims=((1,), (0,))):
    return lax.dot_general(a, b, (dims, ((), ())), preferred_element_type=F32)


def step_kernel(n, sizes, plan, flat, scale, acts_hbm, enc_hbm, dec_hbm, benc_hbm, bdec_hbm, *refs):
    if flat:
        (turned, gpre, gdec, gbenc, gbdec), refs = refs[:5], refs[5:]
        (full, err, feat, feat_turned), refs = refs[:4], refs[4:]
    else:
        (full, err, feat, gpre, gbenc, gbdec), refs = refs[:6], refs[6:]
    (
        enc, dec, benc_ref, bdec_ref, part, own,
        side_out, side_in, line_out, line_in,
        xup_out, xup_in, xdown_out, xdown_in, sum_out, sum_in, total, gate,
        far_in, load_sem, block_send, block_recv, side_sem, line_send, line_recv, cross_sem, far_recv, sum_sem,
    ) = refs
    depth = n // INNER
    tokens, width = acts_hbm.shape
    chunks = len(sizes)
    me = lax.axis_index("latent")
    z, y = me // INNER, lax.rem(me, INNER)
    partner = z * INNER + 1 - y
    layer = lax.axis_index("layer")
    peers = 4
    not_top, not_bottom = z < depth - 1, z > 0

    barrier = pltpu.get_barrier_semaphore()

    def greet(axis, index):
        pl.semaphore_signal(barrier, inc=1, device_id={axis: index}, device_id_type=MESH)

    greet("latent", partner)
    pl.when(not_top)(lambda: greet("latent", me + INNER))
    pl.when(not_bottom)(lambda: greet("latent", me - INNER))
    for k in range(1, peers):
        greet("layer", lax.rem(layer + k, peers))
    loads = [
        pltpu.make_async_copy(acts_hbm, full.at[me], load_sem.at[0]),
        pltpu.make_async_copy(benc_hbm, benc_ref, load_sem.at[1]),
        pltpu.make_async_copy(bdec_hbm, bdec_ref, load_sem.at[2]),
        pltpu.make_async_copy(enc_hbm, enc, load_sem.at[3]),
        pltpu.make_async_copy(dec_hbm, dec, load_sem.at[4]),
    ]
    for load in loads:
        load.start()
    pl.semaphore_wait(
        barrier, peers + jnp.where(not_top, 1, 0) + jnp.where(not_bottom, 1, 0)
    )

    gbdec[...] = jnp.zeros_like(gbdec)
    gbenc[...] = jnp.zeros_like(gbenc)

    starts = [sum(sizes[:c]) for c in range(chunks)]

    def span(c):
        return pl.ds(starts[c], sizes[c])

    steps = plan["chunks"]

    def share(c, peer):
        quarter = sizes[c] // peers
        return pl.ds(pl.multiple_of(starts[c] + peer * quarter, quarter), quarter)

    def slot(c):
        return pl.ds(starts[c] // peers, sizes[c] // peers)

    def enc_rows(b):
        return enc[pl.ds(pl.multiple_of(b * width, width), width), :]

    def dec_columns(b):
        if flat:
            return dec[:, pl.ds(pl.multiple_of(b * width, width), width)]
        return dec[b]

    targets = (partner, me + INNER, me - INNER)

    def at_distance(d, up, use):
        at = z + d if up else z - d
        pl.when(at < depth if up else at >= 0)(lambda: use(at))

    def gather_copy(buf, c, b, way, source=None):
        spot = buf.at[b, span(c), :]
        return remote(
            spot if source is None else source, spot,
            block_send.at[c, b], block_recv.at[c, b], "latent", targets[way],
        )

    def gather_far(buf, c, at, source):
        spot = buf.at[me, span(c), :]
        return remote(
            spot if source is None else source, spot,
            block_send.at[c, me], block_recv.at[c, me], "latent", at * INNER + y,
        )

    def drain(buf, c, b, count, most):
        for k in range(1, most + 1):

            @pl.when(count == k)
            def _():
                spot = buf.at[pl.ds(0, k), span(c), :]
                remote(
                    spot, spot, block_send.at[c, b], block_recv.at[c, b], "latent", partner
                ).wait_send()

    def gather_own(buf, c, chain, source):
        for d in range(depth - 1, chain, -1):
            for up in (True, False):
                at_distance(d, up, lambda at: gather_far(buf, c, at, source).start())
        pl.when(not_top)(lambda: gather_copy(buf, c, me, 1, source).start())
        pl.when(not_bottom)(lambda: gather_copy(buf, c, me, 2, source).start())
        gather_copy(buf, c, me, 0, source).start()

    def gather_line(buf, c, cross, chain, d, below):
        def go(at):
            b = at * INNER + y
            gather_copy(buf, c, b, 0).wait_recv()
            if d < chain:
                way = 1 if below else 2
                pl.when(not_top if below else not_bottom)(lambda: gather_copy(buf, c, b, way).start())
            if not (cross and d == 1):
                gather_copy(buf, c, b, 0).start()

        at_distance(d, not below, go)

    def gather_side(buf, c, cross, d, below):
        def go(at):
            b = at * INNER + 1 - y
            gather_copy(buf, c, b, 0).wait_recv()
            if cross and d == 0:
                pl.when(not_top)(lambda: gather_copy(buf, c, b, 1).start())
                pl.when(not_bottom)(lambda: gather_copy(buf, c, b, 2).start())

        at_distance(d, not below, go)

    def one(condition):
        return jnp.where(condition, 1, 0)

    def gather_drain(buf, c, cross, chain):
        ends = one(not_top) + one(not_bottom)
        count = 1 + ends
        for d in range(chain + 1, depth):
            count = count + one(z + d < depth) + one(z >= d)
        drain(buf, c, me, count, depth + 1)
        for d in range(1, depth):
            for below in (True, False):

                def go(at):
                    count = 0 if cross and d == 1 else 1
                    if d < chain:
                        count = count + one(not_top if below else not_bottom)
                    drain(buf, c, at * INNER + y, count, 2)

                if d < chain or not (cross and d == 1):
                    at_distance(d, not below, go)
        if cross:
            drain(buf, c, partner, ends, 2)

    def on_block(d, below, side, use):
        at = z - d if below else z + d

        @pl.when(at >= 0 if below else at < depth)
        def _():
            use(at * INNER + (1 - y if side else y))

    events = []

    def event(time, function, *args):
        events.append((time, len(events), functools.partial(function, *args)))

    def gather_events(buf, c, cross, chain, source, times, use):
        begin, along, aside = times
        late = plan["use"]
        event(begin, gather_own, buf, c, chain, source)
        event(begin + 0.1, use, c, me)
        last = begin + 0.1
        for d in range(1, depth):
            at = max(along[d - 1], begin + 0.2)
            last = max(last, at + late)
            for below in (True, False):
                event(at, gather_line, buf, c, cross, chain, d, below)
                event(at + late, on_block, d, below, False, functools.partial(use, c))
        for d in range(depth):
            at = max(aside[d], begin + 0.2)
            last = max(last, at + late)
            for below in (True, False) if d else (True,):
                event(at, gather_side, buf, c, cross, d, below)
                event(at + late, on_block, d, below, True, functools.partial(use, c))
        return last + 0.05

    def sum_copy(s, c, phase, k):
        peer = lax.rem(layer + k, peers)
        if phase == 0:
            src = sum_out.at[s, share(c, peer), :]
            dst = sum_in.at[s, k - 1, slot(c), :]
        else:
            src = total.at[s, share(c, layer), :]
            dst = src
        return remote(
            src, dst, sum_sem.at[0, c, phase], sum_sem.at[1, c, phase], "layer", peer,
        )

    def sum_all(s, c, phase):
        spot = sum_in.at[s, :, slot(c), :]
        return remote(
            spot, spot, sum_sem.at[0, c, phase], sum_sem.at[1, c, phase], "layer",
            lax.rem(layer + 1, peers),
        )

    def sum_first(s, c):
        sum_out[s, span(c), :] = part[s, span(c), :].astype(BF16)
        for k in (2, 1, 3):
            sum_copy(s, c, 0, k).start()

    def sum_second(s, c):
        sum_all(s, c, 0).wait_recv()
        mine = share(c, layer)
        value = part[s, mine, :]
        for k in range(1, peers):
            value = value + sum_in[s, k - 1, slot(c), :].astype(F32)
        total[s, mine, :] = value.astype(BF16)
        for k in (2, 1, 3):
            sum_copy(s, c, 1, k).start()

    def sum_third(s, c):
        sum_all(s, c, 1).wait_recv()

    def sum_finish(s, c):
        sum_all(s, c, 0).wait_send()
        sum_all(s, c, 1).wait_send()

    def use_act(c, b):
        value = dot(full[b, span(c), :], enc_rows(b))
        part[0, span(c), :] = value if b is me else part[0, span(c), :] + value

    def use_err(c, b):
        value = dot(err[b, span(c), :], dec_columns(b), ((1,), (1,)))
        part[1, span(c), :] = value if b is me else part[1, span(c), :] + value

    def activate(c):
        sum_third(0, c)
        wide = 4.0 * (total[0, span(c), :].astype(F32) + benc_ref[...])
        soft = jnp.maximum(wide, 0.0) + jnp.log1p(jnp.exp(-jnp.abs(wide)))
        feat[span(c), :] = (soft * 0.25).astype(BF16)

    def open_gate(c):
        wide = 4.0 * (total[0, span(c), :].astype(F32) + benc_ref[...])
        gate[span(c), :] = scale * jax.nn.sigmoid(wide)

    def term(c, b):
        return dot(feat[span(c), :], dec_columns(b))

    def side_copy(c, at):
        return remote(
            side_out.at[at, span(c), :], side_in.at[at, span(c), :],
            side_sem.at[0, c, at], side_sem.at[1, c, at], "latent", partner,
        )

    def land(at, up):
        return at + 1 if up else at

    def line_copy(c, at, up):
        return remote(
            line_out.at[at, span(c), :], line_in.at[land(at, up), span(c), :],
            line_send.at[c, at], line_recv.at[c, land(at, up)],
            "latent", me + INNER if up else me - INNER,
        )

    def far_copy(c, at, source):
        return remote(
            line_out.at[at, span(c), :], far_in.at[source, span(c), :],
            line_send.at[c, at], far_recv.at[c, source], "latent", at * INNER + y,
        )

    def cross_copy(c, up):
        out, spot = (xup_out, xup_in) if up else (xdown_out, xdown_in)
        k = 0 if up else 1
        return remote(
            out.at[span(c), :], spot.at[span(c), :], cross_sem.at[0, c, k], cross_sem.at[1, c, k],
            "latent", me + INNER if up else me - INNER,
        )

    def scatter_other(c, d, up):
        def go(at):
            value = term(c, at * INNER + 1 - y).astype(BF16)
            if steps[c]["cross"][1] and d == 1:
                out = xup_out if up else xdown_out
                out[span(c), :] = value
                cross_copy(c, up).start()
            else:
                side_out[at, span(c), :] = value
                side_copy(c, at).start()

        at_distance(d, up, go)

    def scatter_other_near(c):
        value = term(c, z * INNER + 1 - y)
        if not steps[c]["cross"][1]:
            side_out[z, span(c), :] = value.astype(BF16)
            side_copy(c, z).start()
            return
        own[z, span(c), :] = value
        for up, valid in ((True, not_bottom), (False, not_top)):

            @pl.when(valid)
            def _():
                cross_copy(c, up).wait_recv()
                own[z, span(c), :] = own[z, span(c), :] + (xup_in if up else xdown_in)[span(c), :].astype(F32)

        side_out[z, span(c), :] = own[z, span(c), :].astype(BF16)
        side_copy(c, z).start()

    def scatter_own(c, d, up):
        def go(at):
            own[at, span(c), :] = term(c, at * INNER + y)

        at_distance(d, up, go)

    def scatter_line(c, d, up):
        inner = not_bottom if up else not_top

        def go(at):
            value = own[at, span(c), :]
            if not (steps[c]["cross"][1] and d == 1):
                side_copy(c, at).wait_recv()
                value = value + side_in[at, span(c), :].astype(F32)

            chain = steps[c]["chain"][1]
            if d >= chain:
                line_out[at, span(c), :] = value.astype(BF16)
                (line_copy(c, at, up) if d == chain else far_copy(c, at, z)).start()
                return

            @pl.when(inner)
            def _():
                line_copy(c, at, up).wait_recv()
                line_out[at, span(c), :] = (
                    value + line_in[land(at, up), span(c), :].astype(F32)
                ).astype(BF16)

            @pl.when(jnp.logical_not(inner))
            def _():
                line_out[at, span(c), :] = value.astype(BF16)

            line_copy(c, at, up).start()

        at_distance(d, up, go)

    def scatter_last(c):
        side_copy(c, z).wait_recv()
        value = own[z, span(c), :] + side_in[z, span(c), :].astype(F32)
        own[z, span(c), :] = value + bdec_ref[...].astype(F32) - full[me, span(c), :].astype(F32)
        for up, valid in ((True, not_bottom), (False, not_top)):

            @pl.when(valid)
            def _():
                line_copy(c, z, up).wait_recv()
                own[z, span(c), :] = own[z, span(c), :] + line_in[land(z, up), span(c), :].astype(F32)

        for d in range(steps[c]["chain"][1] + 1, depth):
            for up in (True, False):

                def add(at):
                    far_copy(c, z, at).wait_recv()
                    own[z, span(c), :] = own[z, span(c), :] + far_in[at, span(c), :].astype(F32)

                at_distance(d, up, add)
        value = own[z, span(c), :].astype(BF16)
        err[me, span(c), :] = value
        gbdec[...] = gbdec[...] + scale * jnp.sum(value.astype(F32), axis=0, keepdims=True)

    def scatter_finish(c):
        for d in range(depth - 1, 0, -1):
            for up in (True, False):
                if steps[c]["cross"][1] and d == 1:
                    at_distance(d, up, lambda at: cross_copy(c, up).wait_send())
                else:
                    at_distance(d, up, lambda at: side_copy(c, at).wait_send())
                if d > steps[c]["chain"][1]:
                    at_distance(d, up, lambda at: far_copy(c, at, z).wait_send())
                else:
                    at_distance(d, up, lambda at: line_copy(c, at, up).wait_send())
        side_copy(c, z).wait_send()

    def close(c):
        sum_third(1, c)
        value = total[1, span(c), :].astype(F32) * gate[span(c), :]
        gbenc[...] = gbenc[...] + jnp.sum(value, axis=0, keepdims=True)
        gpre[span(c), :] = value.astype(BF16)

    def own_near(c):
        own[z, span(c), :] = term(c, z * INNER + y)

    def turn(b):
        turned[pl.ds(b * width, width), :] = full[b].T

    def turn_feat():
        feat_turned[...] = feat[...].T

    def finish_dec(b):
        columns = pl.ds(b * width, width)
        gdec[:, columns] = (scale * dot(feat_turned[...], err[b])).astype(BF16)

    source = lambda c: acts_hbm.at[span(c), :]
    event(0.05, loads[0].wait)
    event(0.06, loads[3].wait)
    event(2.0, loads[1].wait)
    event(2.0, loads[2].wait)
    event(2.0, loads[4].wait)
    last = closing = 0.0
    for c in range(chunks):
        step = steps[c]
        ready = gather_events(
            full, c, step["cross"][0], step["chain"][0], source(c), step["act"], use_act

        )
        last = max(last, ready)
        first, second = step["sums"]
        event(ready, sum_first, 0, c)
        event(ready + first, sum_second, 0, c)
        event(ready + first + second, activate, c)
        begin = max(ready + first + second + 0.05, step["out"])
        for d in range(depth - 1, 0, -1):
            for up in (True, False):
                event(begin, scatter_other, c, d, up)
        for d in range(depth - 1, 0, -1):
            for up in (True, False):
                event(begin + 0.2, scatter_own, c, d, up)
                event(max(step["line"][d - 1], begin + 0.3), scatter_line, c, d, up)
        near = max(step["near"], begin + 0.1)
        event(near, scatter_other_near, c)
        mine = max(step["own"], near + 0.01)
        event(mine, own_near, c)
        event(mine, open_gate, c)
        done = max(step["done"], mine + 0.01)
        event(done - 0.005, gather_drain, full, c, step["cross"][0], step["chain"][0])
        event(done, scatter_last, c)
        event(done + 0.005, sum_finish, 0, c)
        times = step["err"]
        ready = gather_events(
            err, c, step["cross"][2], step["chain"][2], None,
            (max(times[0], done + 0.01),) + tuple(times[1:]), use_err
        )
        first, second = step["last_sums"]
        event(ready, sum_first, 1, c)
        event(ready + first, sum_second, 1, c)
        event(ready + first + second, close, c)
        closing = max(closing, ready)
    if flat:
        for b in range(n):
            event(last + 2.0 + b, turn, b)
            event(closing + (0.01 if b < n // 2 else first + 0.01), finish_dec, b)
        event(closing - 1.0, turn_feat)
    for _, _, function in sorted(events, key=lambda e: e[:2]):
        function()
    for c in range(chunks):
        gather_drain(err, c, steps[c]["cross"][2], steps[c]["chain"][2])
        scatter_finish(c)
        sum_finish(1, c)


def write_kernel(n, width, turned, gpre, gdec, gbenc, gbdec, genc_out, gdec_out, gbenc_out, gbdec_out, genc, sem):
    copies = [
        pltpu.make_async_copy(src, dst, sem.at[n + i])
        for i, (src, dst) in enumerate(
            ((gdec, gdec_out), (gbenc, gbenc_out), (gbdec, gbdec_out))
        )
    ]
    for copy in copies:
        copy.start()
    for b in range(n):
        lines = pl.ds(b * width, width)
        genc[lines, :] = dot(turned[lines, :], gpre[...]).astype(BF16)
        copies.append(pltpu.make_async_copy(genc.at[lines, :], genc_out.at[lines, :], sem.at[b]))
        copies[-1].start()
    for copy in copies:
        copy.wait()


def body(n, acts, w_enc, b_enc, w_dec, b_dec):
    local, enc, dec = acts[0], w_enc[0], w_dec[0]
    tokens, width = local.shape
    latents = enc.shape[1]
    depth = n // INNER
    flat = width % 128 == 0 and latents % 128 == 0
    unit = tokens // sum(SHARES)
    if flat and tokens % sum(SHARES) == 0 and unit % 64 == 0:
        sizes = [unit * s for s in SHARES]
    else:
        sizes = [tokens]
    chunks = len(sizes)
    plan = default_plan(depth, chunks)
    if PLAN is not None and chunks == len(SHARES) and depth == len(PLAN["chunks"][0]["line"]) + 1:
        plan = PLAN
    far = any(step["chain"][1] < depth - 1 for step in plan["chunks"])
    scale = tokens ** (-0.5)
    if not flat:
        dec = dec.reshape(latents, n, width).transpose(1, 0, 2)
    vmem = pl.BlockSpec(memory_space=pltpu.VMEM)
    hbm = pl.BlockSpec(memory_space=pl.ANY)
    dma = pltpu.SemaphoreType.DMA
    blocks = (n, tokens, width)
    hidden = (tokens, latents)
    side = pltpu.VMEM((depth, tokens, width), BF16)
    line = pltpu.VMEM((depth + 1, tokens, width), BF16)
    cross = pltpu.VMEM((tokens, width), BF16)
    kind = pltpu.VMEM if flat else jax.ShapeDtypeStruct
    small = (kind((1, latents), F32), kind((1, width), F32))
    inner = (blocks, blocks, hidden, hidden)
    if flat:
        outs = (
            pltpu.VMEM((n * width, tokens), BF16),
            pltpu.VMEM(hidden, BF16),
            pltpu.VMEM((latents, n * width), BF16),
        )
        extra = [pltpu.VMEM(shape, BF16) for shape in (blocks, blocks, hidden, (latents, tokens))]
    else:
        outs = tuple(jax.ShapeDtypeStruct(shape, BF16) for shape in inner)
        extra = []
    results = pl.pallas_call(
        functools.partial(step_kernel, n, sizes, plan, flat, scale),
        out_shape=outs + small,
        in_specs=[hbm] * 5,
        out_specs=(vmem,) * (len(outs) + 2),
        scratch_shapes=extra + [
            pltpu.VMEM(enc.shape, BF16),
            pltpu.VMEM(dec.shape, BF16),
            pltpu.VMEM((1, latents), F32),
            pltpu.VMEM((1, width), BF16),
            pltpu.VMEM((2,) + hidden, F32),
            pltpu.VMEM((depth, tokens, width), F32),
            side, side, line, line,
            cross, cross, cross, cross,
            pltpu.VMEM((2,) + hidden, BF16),
            pltpu.VMEM((2, 3, tokens // 4, latents), BF16),
            pltpu.VMEM((2,) + hidden, BF16),
            pltpu.VMEM(hidden, F32),
            side if far else pltpu.VMEM((1, 16, width), BF16),
            dma((5,)),
            dma((chunks, n)),
            dma((chunks, n)),
            dma((2, chunks, depth)),
            dma((chunks, depth)),
            dma((chunks, depth + 1)),
            dma((2, chunks, 2)),
            dma((chunks, depth)),
            dma((2, chunks, 2)),
        ],
        compiler_params=pltpu.CompilerParams(
            collective_id=0, has_side_effects=True,
            vmem_limit_bytes=VMEM_LIMIT - (4 * n * width * latents if flat else 0),
        ),
        name="step",
    )(local, enc, dec, b_enc[None, :], b_dec)
    gbenc, gbdec = results[-2:]
    if flat:
        held = [pltpu.with_memory_space_constraint(r, pltpu.VMEM) for r in results]
        genc, gdec, gbenc, gbdec = pl.pallas_call(
            functools.partial(write_kernel, n, width),
            out_shape=(
                jax.ShapeDtypeStruct((n * width, latents), BF16),
                jax.ShapeDtypeStruct((latents, n * width), BF16),
            ) + tuple(jax.ShapeDtypeStruct(r.shape, F32) for r in results[-2:]),
            in_specs=[vmem] * 5,
            out_specs=(hbm,) * 4,
            scratch_shapes=[pltpu.VMEM((n * width, latents), BF16), dma((n + 3,))],
            compiler_params=pltpu.CompilerParams(vmem_limit_bytes=8 * n * width * latents),
            name="write",
        )(*held)
    else:
        full, err, feat, gpre = results[:4]
        genc = jnp.einsum("btw,tl->bwl", full, gpre, preferred_element_type=F32)
        genc = genc.astype(BF16).reshape(n * width, latents)
        gdec = jnp.einsum("tl,btw->lbw", feat, err, preferred_element_type=F32)
        gdec = (scale * gdec).astype(BF16).reshape(latents, n * width)
    return genc[None], gdec[None], gbenc[0], gbdec


def solution(mesh):
    return jax.shard_map(
        functools.partial(body, mesh.shape["latent"]),
        mesh=mesh,
        in_specs=(
            P("layer", None, "latent"),
            P("layer", None, "latent"),
            P("latent"),
            P("layer", "latent", None),
            P("layer", "latent"),
        ),
        out_specs=(
            P("layer", None, "latent"),
            P("layer", "latent", None),
            P("latent"),
            P("layer", "latent"),
        ),
        check_vma=False,
    )
```

```python
import functools

import jax
import jax.numpy as jnp
from jax import lax
from jax.experimental import pallas as pl
from jax.experimental.pallas import tpu as pltpu
from jax.sharding import PartitionSpec as P

MESH = pl.DeviceIdType.MESH
F32 = jnp.float32
BF16 = jnp.bfloat16
INNER = 2
VMEM_LIMIT = 60 * 1024 * 1024
SHARES = (1, 1, 1, 1)
PLAN = {'use': 0.01,
 'chunks': [{'act': (0, [0.0, 1.0, 6.5], [7.0, 6.0, 9.2, 14.2]),
             'sums': (7.3, 10.1),
             'out': 30.7,
             'line': [8.1, 46.6, 34.7],
             'near': 42.7,
             'own': 52.3,
             'done': 43.2,
             'err': (54.3, [56.0, 68.8, 78.6], [75.2, 73.6, 79.9, 90.1]),
             'last_sums': (18.2, 59.2),
             'cross': (False, True, False),
             'chain': (3, 1, 3)},
            {'act': (0, [0.5, 3.8, 9.8], [5.2, 12.5, 15.8, 17.7]),
             'sums': (8.4, 7.1),
             'out': 25.8,
             'line': [47.5, 44.5, 43.7],
             'near': 43.3,
             'own': 47.7,
             'done': 54.2,
             'err': (47.7, [55.4, 65.8, 79.9], [73.1, 82.6, 93.9, 91.0]),
             'last_sums': (20.2, 70.1),
             'cross': (True, False, True),
             'chain': (3, 2, 3)},
            {'act': (5.4, [15.6, 24.3, 28.6], [15.3, 25.9, 33.1, 32.6]),
             'sums': (3.8, 9.8),
             'out': 0,
             'line': [66.7, 54.1, 48.6],
             'near': 0.3,
             'own': 70.6,
             'done': 5.3,
             'err': (63.8, [81.1, 90.8, 104.6], [88.3, 109.4, 119.7, 125.6]),
             'last_sums': (25.4, 34.7),
             'cross': (False, False, False),
             'chain': (3, 2, 3)},
            {'act': (0.7, [10.8, 17.7, 25.9], [41.8, 18.9, 26.5, 37.2]),
             'sums': (5.1, 7.1),
             'out': 7.2,
             'line': [70.2, 58.1, 53.3],
             'near': 28.8,
             'own': 11.2,
             'done': 78.9,
             'err': (14.9, [89.5, 96.6, 111.9], [104.4, 137.9, 126.4, 146.6]),
             'last_sums': (26.3, 18.6),
             'cross': (False, False, True),
             'chain': (3, 3, 3)}]}


def default_plan(depth, chunks):
    plan = []
    for c in range(chunks):
        begin, hop = 4.0 * c, 3.0
        act = begin, [begin + d * hop for d in range(1, depth)], [begin + (d + 1) * hop for d in range(depth)]
        out = begin + (depth + 3) * hop
        done = out + (depth + 1) * hop
        err = done, [done + d * hop for d in range(1, depth)], [done + (d + 1) * hop for d in range(depth)]
        plan.append(dict(
            act=act, sums=(hop, hop), out=out, line=[out + (depth - d) * hop for d in range(1, depth)],
            near=out + 0.3, own=out + hop, done=done, err=err, last_sums=(hop, hop),
            cross=(False, False, False), chain=(depth - 1,) * 3,
        ))
    return dict(use=0.3, chunks=plan)


def remote(src, dst, send, recv, axis, index):
    return pltpu.make_async_remote_copy(
        src_ref=src,
        dst_ref=dst,
        send_sem=send,
        recv_sem=recv,
        device_id={axis: index},
        device_id_type=MESH,
    )


def dot(a, b, dims=((1,), (0,))):
    return lax.dot_general(a, b, (dims, ((), ())), preferred_element_type=F32)


def step_kernel(n, sizes, plan, flat, scale, acts_hbm, enc_hbm, dec_hbm, benc_hbm, bdec_hbm, *refs):
    if flat:
        (turned, gpre, gdec, gbenc, gbdec), refs = refs[:5], refs[5:]
        (full, err, feat, feat_turned), refs = refs[:4], refs[4:]
    else:
        (full, err, feat, gpre, gbenc, gbdec), refs = refs[:6], refs[6:]
    (
        enc, dec, benc_ref, bdec_ref, part, own,
        side_out, side_in, line_out, line_in,
        xup_out, xup_in, xdown_out, xdown_in, sum_out, sum_in, total, gate,
        far_in, load_sem, block_send, block_recv, side_sem, line_send, line_recv, cross_sem, far_recv, sum_sem,
    ) = refs
    depth = n // INNER
    tokens, width = acts_hbm.shape
    chunks = len(sizes)
    me = lax.axis_index("latent")
    z, y = me // INNER, lax.rem(me, INNER)
    partner = z * INNER + 1 - y
    layer = lax.axis_index("layer")
    peers = 4
    not_top, not_bottom = z < depth - 1, z > 0

    barrier = pltpu.get_barrier_semaphore()

    def greet(axis, index):
        pl.semaphore_signal(barrier, inc=1, device_id={axis: index}, device_id_type=MESH)

    greet("latent", partner)
    pl.when(not_top)(lambda: greet("latent", me + INNER))
    pl.when(not_bottom)(lambda: greet("latent", me - INNER))
    for k in range(1, peers):
        greet("layer", lax.rem(layer + k, peers))
    loads = [
        pltpu.make_async_copy(acts_hbm, full.at[me], load_sem.at[0]),
        pltpu.make_async_copy(benc_hbm, benc_ref, load_sem.at[1]),
        pltpu.make_async_copy(bdec_hbm, bdec_ref, load_sem.at[2]),
        pltpu.make_async_copy(enc_hbm, enc, load_sem.at[3]),
        pltpu.make_async_copy(dec_hbm, dec, load_sem.at[4]),
    ]
    for load in loads:
        load.start()
    pl.semaphore_wait(
        barrier, peers + jnp.where(not_top, 1, 0) + jnp.where(not_bottom, 1, 0)
    )

    gbdec[...] = jnp.zeros_like(gbdec)
    gbenc[...] = jnp.zeros_like(gbenc)

    starts = [sum(sizes[:c]) for c in range(chunks)]

    def span(c):
        return pl.ds(starts[c], sizes[c])

    steps = plan["chunks"]

    def share(c, peer):
        quarter = sizes[c] // peers
        return pl.ds(pl.multiple_of(starts[c] + peer * quarter, quarter), quarter)

    def slot(c):
        return pl.ds(starts[c] // peers, sizes[c] // peers)

    def enc_rows(b):
        return enc[pl.ds(pl.multiple_of(b * width, width), width), :]

    def dec_columns(b):
        if flat:
            return dec[:, pl.ds(pl.multiple_of(b * width, width), width)]
        return dec[b]

    targets = (partner, me + INNER, me - INNER)

    def at_distance(d, up, use):
        at = z + d if up else z - d
        pl.when(at < depth if up else at >= 0)(lambda: use(at))

    def gather_copy(buf, c, b, way, source=None):
        spot = buf.at[b, span(c), :]
        return remote(
            spot if source is None else source, spot,
            block_send.at[c, b], block_recv.at[c, b], "latent", targets[way],
        )

    def gather_far(buf, c, at, source):
        spot = buf.at[me, span(c), :]
        return remote(
            spot if source is None else source, spot,
            block_send.at[c, me], block_recv.at[c, me], "latent", at * INNER + y,
        )

    def drain(buf, c, b, count, most):
        for k in range(1, most + 1):

            @pl.when(count == k)
            def _():
                spot = buf.at[pl.ds(0, k), span(c), :]
                remote(
                    spot, spot, block_send.at[c, b], block_recv.at[c, b], "latent", partner
                ).wait_send()

    def gather_own(buf, c, chain, source):
        for d in range(depth - 1, chain, -1):
            for up in (True, False):
                at_distance(d, up, lambda at: gather_far(buf, c, at, source).start())
        pl.when(not_top)(lambda: gather_copy(buf, c, me, 1, source).start())
        pl.when(not_bottom)(lambda: gather_copy(buf, c, me, 2, source).start())
        gather_copy(buf, c, me, 0, source).start()

    def gather_line(buf, c, cross, chain, d, below):
        def go(at):
            b = at * INNER + y
            gather_copy(buf, c, b, 0).wait_recv()
            if d < chain:
                way = 1 if below else 2
                pl.when(not_top if below else not_bottom)(lambda: gather_copy(buf, c, b, way).start())
            if not (cross and d == 1):
                gather_copy(buf, c, b, 0).start()

        at_distance(d, not below, go)

    def gather_side(buf, c, cross, d, below):
        def go(at):
            b = at * INNER + 1 - y
            gather_copy(buf, c, b, 0).wait_recv()
            if cross and d == 0:
                pl.when(not_top)(lambda: gather_copy(buf, c, b, 1).start())
                pl.when(not_bottom)(lambda: gather_copy(buf, c, b, 2).start())

        at_distance(d, not below, go)

    def one(condition):
        return jnp.where(condition, 1, 0)

    def gather_drain(buf, c, cross, chain):
        ends = one(not_top) + one(not_bottom)
        count = 1 + ends
        for d in range(chain + 1, depth):
            count = count + one(z + d < depth) + one(z >= d)
        drain(buf, c, me, count, depth + 1)
        for d in range(1, depth):
            for below in (True, False):

                def go(at):
                    count = 0 if cross and d == 1 else 1
                    if d < chain:
                        count = count + one(not_top if below else not_bottom)
                    drain(buf, c, at * INNER + y, count, 2)

                if d < chain or not (cross and d == 1):
                    at_distance(d, not below, go)
        if cross:
            drain(buf, c, partner, ends, 2)

    def on_block(d, below, side, use):
        at = z - d if below else z + d

        @pl.when(at >= 0 if below else at < depth)
        def _():
            use(at * INNER + (1 - y if side else y))

    events = []

    def event(time, function, *args):
        events.append((time, len(events), functools.partial(function, *args)))

    def gather_events(buf, c, cross, chain, source, times, use):
        begin, along, aside = times
        late = plan["use"]
        event(begin, gather_own, buf, c, chain, source)
        event(begin + 0.1, use, c, me)
        last = begin + 0.1
        for d in range(1, depth):
            at = max(along[d - 1], begin + 0.2)
            last = max(last, at + late)
            for below in (True, False):
                event(at, gather_line, buf, c, cross, chain, d, below)
                event(at + late, on_block, d, below, False, functools.partial(use, c))
        for d in range(depth):
            at = max(aside[d], begin + 0.2)
            last = max(last, at + late)
            for below in (True, False) if d else (True,):
                event(at, gather_side, buf, c, cross, d, below)
                event(at + late, on_block, d, below, True, functools.partial(use, c))
        return last + 0.05

    def sum_copy(s, c, phase, k):
        peer = lax.rem(layer + k, peers)
        if phase == 0:
            src = sum_out.at[s, share(c, peer), :]
            dst = sum_in.at[s, k - 1, slot(c), :]
        else:
            src = total.at[s, share(c, layer), :]
            dst = src
        return remote(
            src, dst, sum_sem.at[0, c, phase], sum_sem.at[1, c, phase], "layer", peer,
        )

    def sum_all(s, c, phase):
        spot = sum_in.at[s, :, slot(c), :]
        return remote(
            spot, spot, sum_sem.at[0, c, phase], sum_sem.at[1, c, phase], "layer",
            lax.rem(layer + 1, peers),
        )

    def sum_first(s, c):
        sum_out[s, span(c), :] = part[s, span(c), :].astype(BF16)
        for k in (2, 1, 3):
            sum_copy(s, c, 0, k).start()

    def sum_second(s, c):
        sum_all(s, c, 0).wait_recv()
        mine = share(c, layer)
        value = part[s, mine, :]
        for k in range(1, peers):
            value = value + sum_in[s, k - 1, slot(c), :].astype(F32)
        total[s, mine, :] = value.astype(BF16)
        for k in (2, 1, 3):
            sum_copy(s, c, 1, k).start()

    def sum_third(s, c):
        sum_all(s, c, 1).wait_recv()

    def sum_finish(s, c):
        sum_all(s, c, 0).wait_send()
        sum_all(s, c, 1).wait_send()

    def use_act(c, b):
        value = dot(full[b, span(c), :], enc_rows(b))
        part[0, span(c), :] = value if b is me else part[0, span(c), :] + value

    def use_err(c, b):
        value = dot(err[b, span(c), :], dec_columns(b), ((1,), (1,)))
        part[1, span(c), :] = value if b is me else part[1, span(c), :] + value

    def activate(c):
        sum_third(0, c)
        wide = 4.0 * (total[0, span(c), :].astype(F32) + benc_ref[...])
        soft = jnp.maximum(wide, 0.0) + jnp.log1p(jnp.exp(-jnp.abs(wide)))
        feat[span(c), :] = (soft * 0.25).astype(BF16)

    def open_gate(c):
        wide = 4.0 * (total[0, span(c), :].astype(F32) + benc_ref[...])
        gate[span(c), :] = scale * jax.nn.sigmoid(wide)

    def term(c, b):
        return dot(feat[span(c), :], dec_columns(b))

    def side_copy(c, at):
        return remote(
            side_out.at[at, span(c), :], side_in.at[at, span(c), :],
            side_sem.at[0, c, at], side_sem.at[1, c, at], "latent", partner,
        )

    def land(at, up):
        return at + 1 if up else at

    def line_copy(c, at, up):
        return remote(
            line_out.at[at, span(c), :], line_in.at[land(at, up), span(c), :],
            line_send.at[c, at], line_recv.at[c, land(at, up)],
            "latent", me + INNER if up else me - INNER,
        )

    def far_copy(c, at, source):
        return remote(
            line_out.at[at, span(c), :], far_in.at[source, span(c), :],
            line_send.at[c, at], far_recv.at[c, source], "latent", at * INNER + y,
        )

    def cross_copy(c, up):
        out, spot = (xup_out, xup_in) if up else (xdown_out, xdown_in)
        k = 0 if up else 1
        return remote(
            out.at[span(c), :], spot.at[span(c), :], cross_sem.at[0, c, k], cross_sem.at[1, c, k],
            "latent", me + INNER if up else me - INNER,
        )

    def scatter_other(c, d, up):
        def go(at):
            value = term(c, at * INNER + 1 - y).astype(BF16)
            if steps[c]["cross"][1] and d == 1:
                out = xup_out if up else xdown_out
                out[span(c), :] = value
                cross_copy(c, up).start()
            else:
                side_out[at, span(c), :] = value
                side_copy(c, at).start()

        at_distance(d, up, go)

    def scatter_other_near(c):
        value = term(c, z * INNER + 1 - y)
        if not steps[c]["cross"][1]:
            side_out[z, span(c), :] = value.astype(BF16)
            side_copy(c, z).start()
            return
        own[z, span(c), :] = value
        for up, valid in ((True, not_bottom), (False, not_top)):

            @pl.when(valid)
            def _():
                cross_copy(c, up).wait_recv()
                own[z, span(c), :] = own[z, span(c), :] + (xup_in if up else xdown_in)[span(c), :].astype(F32)

        side_out[z, span(c), :] = own[z, span(c), :].astype(BF16)
        side_copy(c, z).start()

    def scatter_own(c, d, up):
        def go(at):
            own[at, span(c), :] = term(c, at * INNER + y)

        at_distance(d, up, go)

    def scatter_line(c, d, up):
        inner = not_bottom if up else not_top

        def go(at):
            value = own[at, span(c), :]
            if not (steps[c]["cross"][1] and d == 1):
                side_copy(c, at).wait_recv()
                value = value + side_in[at, span(c), :].astype(F32)

            chain = steps[c]["chain"][1]
            if d >= chain:
                line_out[at, span(c), :] = value.astype(BF16)
                (line_copy(c, at, up) if d == chain else far_copy(c, at, z)).start()
                return

            @pl.when(inner)
            def _():
                line_copy(c, at, up).wait_recv()
                line_out[at, span(c), :] = (
                    value + line_in[land(at, up), span(c), :].astype(F32)
                ).astype(BF16)

            @pl.when(jnp.logical_not(inner))
            def _():
                line_out[at, span(c), :] = value.astype(BF16)

            line_copy(c, at, up).start()

        at_distance(d, up, go)

    def scatter_last(c):
        side_copy(c, z).wait_recv()
        value = own[z, span(c), :] + side_in[z, span(c), :].astype(F32)
        own[z, span(c), :] = value + bdec_ref[...].astype(F32) - full[me, span(c), :].astype(F32)
        for up, valid in ((True, not_bottom), (False, not_top)):

            @pl.when(valid)
            def _():
                line_copy(c, z, up).wait_recv()
                own[z, span(c), :] = own[z, span(c), :] + line_in[land(z, up), span(c), :].astype(F32)

        for d in range(steps[c]["chain"][1] + 1, depth):
            for up in (True, False):

                def add(at):
                    far_copy(c, z, at).wait_recv()
                    own[z, span(c), :] = own[z, span(c), :] + far_in[at, span(c), :].astype(F32)

                at_distance(d, up, add)
        value = own[z, span(c), :].astype(BF16)
        err[me, span(c), :] = value
        gbdec[...] = gbdec[...] + scale * jnp.sum(value.astype(F32), axis=0, keepdims=True)

    def scatter_finish(c):
        for d in range(depth - 1, 0, -1):
            for up in (True, False):
                if steps[c]["cross"][1] and d == 1:
                    at_distance(d, up, lambda at: cross_copy(c, up).wait_send())
                else:
                    at_distance(d, up, lambda at: side_copy(c, at).wait_send())
                if d > steps[c]["chain"][1]:
                    at_distance(d, up, lambda at: far_copy(c, at, z).wait_send())
                else:
                    at_distance(d, up, lambda at: line_copy(c, at, up).wait_send())
        side_copy(c, z).wait_send()

    def close(c):
        sum_third(1, c)
        value = total[1, span(c), :].astype(F32) * gate[span(c), :]
        gbenc[...] = gbenc[...] + jnp.sum(value, axis=0, keepdims=True)
        gpre[span(c), :] = value.astype(BF16)

    def own_near(c):
        own[z, span(c), :] = term(c, z * INNER + y)

    def turn(b):
        turned[pl.ds(b * width, width), :] = full[b].T

    def turn_feat():
        feat_turned[...] = feat[...].T

    def finish_dec(b):
        columns = pl.ds(b * width, width)
        gdec[:, columns] = (scale * dot(feat_turned[...], err[b])).astype(BF16)

    source = lambda c: acts_hbm.at[span(c), :]
    event(0.05, loads[0].wait)
    event(0.06, loads[3].wait)
    event(2.0, loads[1].wait)
    event(2.0, loads[2].wait)
    event(2.0, loads[4].wait)
    last = closing = 0.0
    for c in range(chunks):
        step = steps[c]
        ready = gather_events(
            full, c, step["cross"][0], step["chain"][0], source(c), step["act"], use_act

        )
        last = max(last, ready)
        first, second = step["sums"]
        event(ready, sum_first, 0, c)
        event(ready + first, sum_second, 0, c)
        event(ready + first + second, activate, c)
        begin = max(ready + first + second + 0.05, step["out"])
        for d in range(depth - 1, 0, -1):
            for up in (True, False):
                event(begin, scatter_other, c, d, up)
        for d in range(depth - 1, 0, -1):
            for up in (True, False):
                event(begin + 0.2, scatter_own, c, d, up)
                event(max(step["line"][d - 1], begin + 0.3), scatter_line, c, d, up)
        near = max(step["near"], begin + 0.1)
        event(near, scatter_other_near, c)
        mine = max(step["own"], near + 0.01)
        event(mine, own_near, c)
        event(mine, open_gate, c)
        event(mine, gather_drain, full, c, step["cross"][0], step["chain"][0])
        event(mine, sum_finish, 0, c)
        done = max(step["done"], mine + 0.01)
        event(done, scatter_last, c)
        times = step["err"]
        ready = gather_events(
            err, c, step["cross"][2], step["chain"][2], None,
            (max(times[0], done + 0.01),) + tuple(times[1:]), use_err
        )
        first, second = step["last_sums"]
        event(ready, sum_first, 1, c)
        event(ready + first, sum_second, 1, c)
        event(ready + first + 0.005, scatter_finish, c)
        event(ready + first + 0.005, gather_drain, err, c, step["cross"][2], step["chain"][2])
        event(ready + first + second, close, c)
        closing = max(closing, ready)
    if flat:
        for b in range(n):
            event(last + 2.0 + b, turn, b)
            event(closing + (0.01 if b < n // 2 else first + 0.01), finish_dec, b)
        event(closing - 1.0, turn_feat)
    for _, _, function in sorted(events, key=lambda e: e[:2]):
        function()
    for c in range(chunks):
        sum_finish(1, c)


def write_kernel(n, width, turned, gpre, gdec, gbenc, gbdec, genc_out, gdec_out, gbenc_out, gbdec_out, genc, sem):
    copies = [
        pltpu.make_async_copy(src, dst, sem.at[n + i])
        for i, (src, dst) in enumerate(
            ((gdec, gdec_out), (gbenc, gbenc_out), (gbdec, gbdec_out))
        )
    ]
    for copy in copies:
        copy.start()
    for b in range(n):
        lines = pl.ds(b * width, width)
        genc[lines, :] = dot(turned[lines, :], gpre[...]).astype(BF16)
        copies.append(pltpu.make_async_copy(genc.at[lines, :], genc_out.at[lines, :], sem.at[b]))
        copies[-1].start()
    for copy in copies:
        copy.wait()


def body(n, acts, w_enc, b_enc, w_dec, b_dec):
    local, enc, dec = acts[0], w_enc[0], w_dec[0]
    tokens, width = local.shape
    latents = enc.shape[1]
    depth = n // INNER
    flat = width % 128 == 0 and latents % 128 == 0
    unit = tokens // sum(SHARES)
    if flat and tokens % sum(SHARES) == 0 and unit % 64 == 0:
        sizes = [unit * s for s in SHARES]
    else:
        sizes = [tokens]
    chunks = len(sizes)
    plan = default_plan(depth, chunks)
    if PLAN is not None and chunks == len(SHARES) and depth == len(PLAN["chunks"][0]["line"]) + 1:
        plan = PLAN
    far = any(step["chain"][1] < depth - 1 for step in plan["chunks"])
    scale = tokens ** (-0.5)
    if not flat:
        dec = dec.reshape(latents, n, width).transpose(1, 0, 2)
    vmem = pl.BlockSpec(memory_space=pltpu.VMEM)
    hbm = pl.BlockSpec(memory_space=pl.ANY)
    dma = pltpu.SemaphoreType.DMA
    blocks = (n, tokens, width)
    hidden = (tokens, latents)
    side = pltpu.VMEM((depth, tokens, width), BF16)
    line = pltpu.VMEM((depth + 1, tokens, width), BF16)
    cross = pltpu.VMEM((tokens, width), BF16)
    kind = pltpu.VMEM if flat else jax.ShapeDtypeStruct
    small = (kind((1, latents), F32), kind((1, width), F32))
    inner = (blocks, blocks, hidden, hidden)
    if flat:
        outs = (
            pltpu.VMEM((n * width, tokens), BF16),
            pltpu.VMEM(hidden, BF16),
            pltpu.VMEM((latents, n * width), BF16),
        )
        extra = [pltpu.VMEM(shape, BF16) for shape in (blocks, blocks, hidden, (latents, tokens))]
    else:
        outs = tuple(jax.ShapeDtypeStruct(shape, BF16) for shape in inner)
        extra = []
    results = pl.pallas_call(
        functools.partial(step_kernel, n, sizes, plan, flat, scale),
        out_shape=outs + small,
        in_specs=[hbm] * 5,
        out_specs=(vmem,) * (len(outs) + 2),
        scratch_shapes=extra + [
            pltpu.VMEM(enc.shape, BF16),
            pltpu.VMEM(dec.shape, BF16),
            pltpu.VMEM((1, latents), F32),
            pltpu.VMEM((1, width), BF16),
            pltpu.VMEM((2,) + hidden, F32),
            pltpu.VMEM((depth, tokens, width), F32),
            side, side, line, line,
            cross, cross, cross, cross,
            pltpu.VMEM((2,) + hidden, BF16),
            pltpu.VMEM((2, 3, tokens // 4, latents), BF16),
            pltpu.VMEM((2,) + hidden, BF16),
            pltpu.VMEM(hidden, F32),
            side if far else pltpu.VMEM((1, 16, width), BF16),
            dma((5,)),
            dma((chunks, n)),
            dma((chunks, n)),
            dma((2, chunks, depth)),
            dma((chunks, depth)),
            dma((chunks, depth + 1)),
            dma((2, chunks, 2)),
            dma((chunks, depth)),
            dma((2, chunks, 2)),
        ],
        compiler_params=pltpu.CompilerParams(
            collective_id=0, has_side_effects=True,
            vmem_limit_bytes=VMEM_LIMIT - (4 * n * width * latents if flat else 0),
        ),
        name="step",
    )(local, enc, dec, b_enc[None, :], b_dec)
    gbenc, gbdec = results[-2:]
    if flat:
        held = [pltpu.with_memory_space_constraint(r, pltpu.VMEM) for r in results]
        genc, gdec, gbenc, gbdec = pl.pallas_call(
            functools.partial(write_kernel, n, width),
            out_shape=(
                jax.ShapeDtypeStruct((n * width, latents), BF16),
                jax.ShapeDtypeStruct((latents, n * width), BF16),
            ) + tuple(jax.ShapeDtypeStruct(r.shape, F32) for r in results[-2:]),
            in_specs=[vmem] * 5,
            out_specs=(hbm,) * 4,
            scratch_shapes=[pltpu.VMEM((n * width, latents), BF16), dma((n + 3,))],
            compiler_params=pltpu.CompilerParams(vmem_limit_bytes=8 * n * width * latents),
            name="write",
        )(*held)
    else:
        full, err, feat, gpre = results[:4]
        genc = jnp.einsum("btw,tl->bwl", full, gpre, preferred_element_type=F32)
        genc = genc.astype(BF16).reshape(n * width, latents)
        gdec = jnp.einsum("tl,btw->lbw", feat, err, preferred_element_type=F32)
        gdec = (scale * gdec).astype(BF16).reshape(latents, n * width)
    return genc[None], gdec[None], gbenc[0], gbdec


def solution(mesh):
    return jax.shard_map(
        functools.partial(body, mesh.shape["latent"]),
        mesh=mesh,
        in_specs=(
            P("layer", None, "latent"),
            P("layer", None, "latent"),
            P("latent"),
            P("layer", "latent", None),
            P("layer", "latent"),
        ),
        out_specs=(
            P("layer", None, "latent"),
            P("layer", "latent", None),
            P("latent"),
            P("layer", "latent"),
        ),
        check_vma=False,
    )
```

```python
import functools

import jax
import jax.numpy as jnp
from jax import lax
from jax.experimental import pallas as pl
from jax.experimental.pallas import tpu as pltpu
from jax.sharding import PartitionSpec as P

MESH = pl.DeviceIdType.MESH
F32 = jnp.float32
BF16 = jnp.bfloat16
INNER = 2
VMEM_LIMIT = 60 * 1024 * 1024
SHARES = (1, 1, 1, 1)
PLAN = {'use': 0.01,
 'chunks': [{'act': (3.4, [5.5, 18.8, 25.2], [21.1, 27.7, 28.9, 30.0]),
             'sums': (0.2, 10.3, 4.1),
             'out': 35.4,
             'line': [9.2, 52.2, 56.5],
             'near': 52.7,
             'own': 60.0,
             'done': 8.8,
             'err': (14.6, [70.1, 77.1, 82.9], [91.1, 83.7, 97.0, 104.5]),
             'last_sums': (6.2, 32.6, 42.9),
             'cross': (True, True, False),
             'chain': (3, 1, 3)},
            {'act': (0, [4.5, 6.5, 12.2], [5.8, 8.4, 21.9, 23.5]),
             'sums': (2.5, 4.1, 2.2),
             'out': 21.8,
             'line': [46.2, 44.5, 39.3],
             'near': 23.3,
             'own': 5.3,
             'done': 55.5,
             'err': (19.4, [57.4, 64.6, 81.1], [73.2, 80.4, 98.7, 97.8]),
             'last_sums': (9.4, 32.9, 68.9),
             'cross': (False, False, False),
             'chain': (3, 2, 3)},
            {'act': (0, [5.0, 9.5, 23.5], [21.5, 10.5, 27.9, 27.6]),
             'sums': (6.4, 10.5, 3.2),
             'out': 22.8,
             'line': [71.2, 62.3, 57.2],
             'near': 61.2,
             'own': 78.8,
             'done': 71.9,
             'err': (3.3, [101.4, 110.7, 103.7], [102.7, 119.1, 134.1, 126.1]),
             'last_sums': (37.7, 36.6, 34.2),
             'cross': (False, True, False),
             'chain': (3, 3, 2)},
            {'act': (9.2, [25.7, 30.1, 31.9], [24.3, 44.0, 36.1, 43.7]),
             'sums': (1.6, 5.6, 5.9),
             'out': 37.2,
             'line': [73.3, 68.1, 56.0],
             'near': 41.6,
             'own': 13.9,
             'done': 82.0,
             'err': (59.8, [107.1, 117.8, 119.3], [116.1, 173.1, 162.1, 179.1]),
             'last_sums': (29.2, 9.7, 52.4),
             'cross': (False, False, True),
             'chain': (3, 3, 2)}]}


def default_plan(depth, chunks):
    plan = []
    for c in range(chunks):
        begin, hop = 4.0 * c, 3.0
        act = begin, [begin + d * hop for d in range(1, depth)], [begin + (d + 1) * hop for d in range(depth)]
        out = begin + (depth + 3) * hop
        done = out + (depth + 1) * hop
        err = done, [done + d * hop for d in range(1, depth)], [done + (d + 1) * hop for d in range(depth)]
        plan.append(dict(
            act=act, sums=(hop / 2, hop, hop / 2), out=out, line=[out + (depth - d) * hop for d in range(1, depth)],
            near=out + 0.3, own=out + hop, done=done, err=err, last_sums=(hop / 2, hop, hop / 2),
            cross=(False, False, False), chain=(depth - 1,) * 3,
        ))
    return dict(use=0.3, chunks=plan)


def remote(src, dst, send, recv, axis, index):
    return pltpu.make_async_remote_copy(
        src_ref=src,
        dst_ref=dst,
        send_sem=send,
        recv_sem=recv,
        device_id={axis: index},
        device_id_type=MESH,
    )


def dot(a, b, dims=((1,), (0,))):
    return lax.dot_general(a, b, (dims, ((), ())), preferred_element_type=F32)


def step_kernel(n, sizes, plan, flat, scale, acts_hbm, enc_hbm, dec_hbm, benc_hbm, bdec_hbm, *refs):
    if flat:
        (turned, gpre, gdec, gbenc, gbdec), refs = refs[:5], refs[5:]
        (full, err, feat, feat_turned), refs = refs[:4], refs[4:]
    else:
        (full, err, feat, gpre, gbenc, gbdec), refs = refs[:6], refs[6:]
    (
        enc, dec, benc_ref, bdec_ref, part, own,
        side_out, side_in, line_out, line_in,
        xup_out, xup_in, xdown_out, xdown_in, sum_out, sum_in, total, gate,
        far_in, load_sem, block_send, block_recv, side_sem, line_send, line_recv, cross_sem, far_recv, sum_sem,
    ) = refs
    depth = n // INNER
    tokens, width = acts_hbm.shape
    chunks = len(sizes)
    me = lax.axis_index("latent")
    z, y = me // INNER, lax.rem(me, INNER)
    partner = z * INNER + 1 - y
    layer = lax.axis_index("layer")
    core = lax.rem(layer, 2)
    twin, opposite = layer + 1 - 2 * core, lax.rem(layer + 2, 4)
    not_top, not_bottom = z < depth - 1, z > 0

    barrier = pltpu.get_barrier_semaphore()

    def greet(axis, index):
        pl.semaphore_signal(barrier, inc=1, device_id={axis: index}, device_id_type=MESH)

    greet("latent", partner)
    pl.when(not_top)(lambda: greet("latent", me + INNER))
    pl.when(not_bottom)(lambda: greet("latent", me - INNER))
    greet("layer", twin)
    greet("layer", opposite)
    loads = [
        pltpu.make_async_copy(acts_hbm, full.at[me], load_sem.at[0]),
        pltpu.make_async_copy(benc_hbm, benc_ref, load_sem.at[1]),
        pltpu.make_async_copy(bdec_hbm, bdec_ref, load_sem.at[2]),
        pltpu.make_async_copy(enc_hbm, enc, load_sem.at[3]),
        pltpu.make_async_copy(dec_hbm, dec, load_sem.at[4]),
    ]
    for load in loads:
        load.start()
    pl.semaphore_wait(
        barrier, 3 + jnp.where(not_top, 1, 0) + jnp.where(not_bottom, 1, 0)
    )

    gbdec[...] = jnp.zeros_like(gbdec)
    gbenc[...] = jnp.zeros_like(gbenc)

    starts = [sum(sizes[:c]) for c in range(chunks)]

    def span(c):
        return pl.ds(starts[c], sizes[c])

    steps = plan["chunks"]

    def half(c, k):
        size = sizes[c] // 2
        return pl.ds(pl.multiple_of(starts[c] + k * size, size), size)

    def slot(c):
        return pl.ds(starts[c] // 2, sizes[c] // 2)

    def enc_rows(b):
        return enc[pl.ds(pl.multiple_of(b * width, width), width), :]

    def dec_columns(b):
        if flat:
            return dec[:, pl.ds(pl.multiple_of(b * width, width), width)]
        return dec[b]

    targets = (partner, me + INNER, me - INNER)

    def at_distance(d, up, use):
        at = z + d if up else z - d
        pl.when(at < depth if up else at >= 0)(lambda: use(at))

    def gather_copy(buf, c, b, way, source=None):
        spot = buf.at[b, span(c), :]
        return remote(
            spot if source is None else source, spot,
            block_send.at[c, b], block_recv.at[c, b], "latent", targets[way],
        )

    def gather_far(buf, c, at, source):
        spot = buf.at[me, span(c), :]
        return remote(
            spot if source is None else source, spot,
            block_send.at[c, me], block_recv.at[c, me], "latent", at * INNER + y,
        )

    def drain(buf, c, b, count, most):
        for k in range(1, most + 1):

            @pl.when(count == k)
            def _():
                spot = buf.at[pl.ds(0, k), span(c), :]
                remote(
                    spot, spot, block_send.at[c, b], block_recv.at[c, b], "latent", partner
                ).wait_send()

    def gather_own(buf, c, chain, source):
        for d in range(depth - 1, chain, -1):
            for up in (True, False):
                at_distance(d, up, lambda at: gather_far(buf, c, at, source).start())
        pl.when(not_top)(lambda: gather_copy(buf, c, me, 1, source).start())
        pl.when(not_bottom)(lambda: gather_copy(buf, c, me, 2, source).start())
        gather_copy(buf, c, me, 0, source).start()

    def gather_line(buf, c, cross, chain, d, below):
        def go(at):
            b = at * INNER + y
            gather_copy(buf, c, b, 0).wait_recv()
            if d < chain:
                way = 1 if below else 2
                pl.when(not_top if below else not_bottom)(lambda: gather_copy(buf, c, b, way).start())
            if not (cross and d == 1):
                gather_copy(buf, c, b, 0).start()

        at_distance(d, not below, go)

    def gather_side(buf, c, cross, d, below):
        def go(at):
            b = at * INNER + 1 - y
            gather_copy(buf, c, b, 0).wait_recv()
            if cross and d == 0:
                pl.when(not_top)(lambda: gather_copy(buf, c, b, 1).start())
                pl.when(not_bottom)(lambda: gather_copy(buf, c, b, 2).start())

        at_distance(d, not below, go)

    def one(condition):
        return jnp.where(condition, 1, 0)

    def gather_drain(buf, c, cross, chain):
        ends = one(not_top) + one(not_bottom)
        count = 1 + ends
        for d in range(chain + 1, depth):
            count = count + one(z + d < depth) + one(z >= d)
        drain(buf, c, me, count, depth + 1)
        for d in range(1, depth):
            for below in (True, False):

                def go(at):
                    count = 0 if cross and d == 1 else 1
                    if d < chain:
                        count = count + one(not_top if below else not_bottom)
                    drain(buf, c, at * INNER + y, count, 2)

                if d < chain or not (cross and d == 1):
                    at_distance(d, not below, go)
        if cross:
            drain(buf, c, partner, ends, 2)

    def on_block(d, below, side, use):
        at = z - d if below else z + d

        @pl.when(at >= 0 if below else at < depth)
        def _():
            use(at * INNER + (1 - y if side else y))

    events = []

    def event(time, function, *args):
        events.append((time, len(events), functools.partial(function, *args)))

    def gather_events(buf, c, cross, chain, source, times, use):
        begin, along, aside = times
        late = plan["use"]
        event(begin, gather_own, buf, c, chain, source)
        event(begin + 0.1, use, c, me)
        last = begin + 0.1
        for d in range(1, depth):
            at = max(along[d - 1], begin + 0.2)
            last = max(last, at + late)
            for below in (True, False):
                event(at, gather_line, buf, c, cross, chain, d, below)
                event(at + late, on_block, d, below, False, functools.partial(use, c))
        for d in range(depth):
            at = max(aside[d], begin + 0.2)
            last = max(last, at + late)
            for below in (True, False) if d else (True,):
                event(at, gather_side, buf, c, cross, d, below)
                event(at + late, on_block, d, below, True, functools.partial(use, c))
        return last + 0.05

    def sum_copy(s, c, phase):
        if phase == 0:
            src, dst = sum_out.at[s, half(c, 1 - core), :], sum_in.at[s, 0, slot(c), :]
        elif phase == 1:
            src, dst = sum_out.at[s, half(c, core), :], sum_in.at[s, 1, slot(c), :]
        else:
            src = dst = total.at[s, half(c, core), :]
        mark = 3 if phase == 1 and s else phase
        return remote(
            src, dst, sum_sem.at[0, c, mark], sum_sem.at[1, c, mark],
            "layer", opposite if phase == 1 else twin,
        )

    def sum_first(s, c):
        sum_out[s, half(c, 1 - core), :] = part[s, half(c, 1 - core), :].astype(BF16)
        sum_copy(s, c, 0).start()

    def sum_second(s, c):
        sum_copy(s, c, 0).wait_recv()
        value = part[s, half(c, core), :] + sum_in[s, 0, slot(c), :].astype(F32)
        sum_out[s, half(c, core), :] = value.astype(BF16)
        sum_copy(s, c, 1).start()

    def sum_third(s, c):
        sum_copy(s, c, 1).wait_recv()
        value = sum_out[s, half(c, core), :].astype(F32) + sum_in[s, 1, slot(c), :].astype(F32)
        total[s, half(c, core), :] = value.astype(BF16)
        sum_copy(s, c, 2).start()

    def sum_fourth(s, c):
        sum_copy(s, c, 2).wait_recv()

    def sum_finish(s, c):
        for phase in range(3):
            sum_copy(s, c, phase).wait_send()

    def use_act(c, b):
        value = dot(full[b, span(c), :], enc_rows(b))
        part[0, span(c), :] = value if b is me else part[0, span(c), :] + value

    def use_err(c, b):
        value = dot(err[b, span(c), :], dec_columns(b), ((1,), (1,)))
        part[1, span(c), :] = value if b is me else part[1, span(c), :] + value

    def activate(c):
        sum_fourth(0, c)
        wide = 4.0 * (total[0, span(c), :].astype(F32) + benc_ref[...])
        soft = jnp.maximum(wide, 0.0) + jnp.log1p(jnp.exp(-jnp.abs(wide)))
        feat[span(c), :] = (soft * 0.25).astype(BF16)

    def open_gate(c):
        wide = 4.0 * (total[0, span(c), :].astype(F32) + benc_ref[...])
        gate[span(c), :] = scale * jax.nn.sigmoid(wide)

    def term(c, b):
        return dot(feat[span(c), :], dec_columns(b))

    def side_copy(c, at):
        return remote(
            side_out.at[at, span(c), :], side_in.at[at, span(c), :],
            side_sem.at[0, c, at], side_sem.at[1, c, at], "latent", partner,
        )

    def land(at, up):
        return at + 1 if up else at

    def line_copy(c, at, up):
        return remote(
            line_out.at[at, span(c), :], line_in.at[land(at, up), span(c), :],
            line_send.at[c, at], line_recv.at[c, land(at, up)],
            "latent", me + INNER if up else me - INNER,
        )

    def far_copy(c, at, source):
        return remote(
            line_out.at[at, span(c), :], far_in.at[source, span(c), :],
            line_send.at[c, at], far_recv.at[c, source], "latent", at * INNER + y,
        )

    def cross_copy(c, up):
        out, spot = (xup_out, xup_in) if up else (xdown_out, xdown_in)
        k = 0 if up else 1
        return remote(
            out.at[span(c), :], spot.at[span(c), :], cross_sem.at[0, c, k], cross_sem.at[1, c, k],
            "latent", me + INNER if up else me - INNER,
        )

    def scatter_other(c, d, up):
        def go(at):
            value = term(c, at * INNER + 1 - y).astype(BF16)
            if steps[c]["cross"][1] and d == 1:
                out = xup_out if up else xdown_out
                out[span(c), :] = value
                cross_copy(c, up).start()
            else:
                side_out[at, span(c), :] = value
                side_copy(c, at).start()

        at_distance(d, up, go)

    def scatter_other_near(c):
        value = term(c, z * INNER + 1 - y)
        if not steps[c]["cross"][1]:
            side_out[z, span(c), :] = value.astype(BF16)
            side_copy(c, z).start()
            return
        own[z, span(c), :] = value
        for up, valid in ((True, not_bottom), (False, not_top)):

            @pl.when(valid)
            def _():
                cross_copy(c, up).wait_recv()
                own[z, span(c), :] = own[z, span(c), :] + (xup_in if up else xdown_in)[span(c), :].astype(F32)

        side_out[z, span(c), :] = own[z, span(c), :].astype(BF16)
        side_copy(c, z).start()

    def scatter_own(c, d, up):
        def go(at):
            own[at, span(c), :] = term(c, at * INNER + y)

        at_distance(d, up, go)

    def scatter_line(c, d, up):
        inner = not_bottom if up else not_top

        def go(at):
            value = own[at, span(c), :]
            if not (steps[c]["cross"][1] and d == 1):
                side_copy(c, at).wait_recv()
                value = value + side_in[at, span(c), :].astype(F32)

            chain = steps[c]["chain"][1]
            if d >= chain:
                line_out[at, span(c), :] = value.astype(BF16)
                (line_copy(c, at, up) if d == chain else far_copy(c, at, z)).start()
                return

            @pl.when(inner)
            def _():
                line_copy(c, at, up).wait_recv()
                line_out[at, span(c), :] = (
                    value + line_in[land(at, up), span(c), :].astype(F32)
                ).astype(BF16)

            @pl.when(jnp.logical_not(inner))
            def _():
                line_out[at, span(c), :] = value.astype(BF16)

            line_copy(c, at, up).start()

        at_distance(d, up, go)

    def scatter_last(c):
        side_copy(c, z).wait_recv()
        value = own[z, span(c), :] + side_in[z, span(c), :].astype(F32)
        own[z, span(c), :] = value + bdec_ref[...].astype(F32) - full[me, span(c), :].astype(F32)
        for up, valid in ((True, not_bottom), (False, not_top)):

            @pl.when(valid)
            def _():
                line_copy(c, z, up).wait_recv()
                own[z, span(c), :] = own[z, span(c), :] + line_in[land(z, up), span(c), :].astype(F32)

        for d in range(steps[c]["chain"][1] + 1, depth):
            for up in (True, False):

                def add(at):
                    far_copy(c, z, at).wait_recv()
                    own[z, span(c), :] = own[z, span(c), :] + far_in[at, span(c), :].astype(F32)

                at_distance(d, up, add)
        value = own[z, span(c), :].astype(BF16)
        err[me, span(c), :] = value
        gbdec[...] = gbdec[...] + scale * jnp.sum(value.astype(F32), axis=0, keepdims=True)

    def scatter_finish(c):
        for d in range(depth - 1, 0, -1):
            for up in (True, False):
                if steps[c]["cross"][1] and d == 1:
                    at_distance(d, up, lambda at: cross_copy(c, up).wait_send())
                else:
                    at_distance(d, up, lambda at: side_copy(c, at).wait_send())
                if d > steps[c]["chain"][1]:
                    at_distance(d, up, lambda at: far_copy(c, at, z).wait_send())
                else:
                    at_distance(d, up, lambda at: line_copy(c, at, up).wait_send())
        side_copy(c, z).wait_send()

    def close(c):
        sum_fourth(1, c)
        value = total[1, span(c), :].astype(F32) * gate[span(c), :]
        gbenc[...] = gbenc[...] + jnp.sum(value, axis=0, keepdims=True)
        gpre[span(c), :] = value.astype(BF16)

    def own_near(c):
        own[z, span(c), :] = term(c, z * INNER + y)

    def turn(b):
        turned[pl.ds(b * width, width), :] = full[b].T

    def turn_feat():
        feat_turned[...] = feat[...].T

    def finish_dec(b):
        columns = pl.ds(b * width, width)
        gdec[:, columns] = (scale * dot(feat_turned[...], err[b])).astype(BF16)

    source = lambda c: acts_hbm.at[span(c), :]
    event(0.05, loads[0].wait)
    event(0.06, loads[3].wait)
    event(2.0, loads[1].wait)
    event(2.0, loads[2].wait)
    event(2.0, loads[4].wait)
    last = closing = 0.0
    for c in range(chunks):
        step = steps[c]
        ready = gather_events(
            full, c, step["cross"][0], step["chain"][0], source(c), step["act"], use_act

        )
        last = max(last, ready)
        first, second, third = step["sums"]
        event(ready, sum_first, 0, c)
        event(ready + first, sum_second, 0, c)
        event(ready + first + second, sum_third, 0, c)
        ready = ready + first + second + third
        event(ready, activate, c)
        begin = max(ready + 0.05, step["out"])
        for d in range(depth - 1, 0, -1):
            for up in (True, False):
                event(begin, scatter_other, c, d, up)
        for d in range(depth - 1, 0, -1):
            for up in (True, False):
                event(begin + 0.2, scatter_own, c, d, up)
                event(max(step["line"][d - 1], begin + 0.3), scatter_line, c, d, up)
        near = max(step["near"], begin + 0.1)
        event(near, scatter_other_near, c)
        mine = max(step["own"], near + 0.01)
        event(mine, own_near, c)
        event(mine, open_gate, c)
        event(mine, gather_drain, full, c, step["cross"][0], step["chain"][0])
        event(mine, sum_finish, 0, c)
        done = max(step["done"], mine + 0.01)
        event(done, scatter_last, c)
        times = step["err"]
        ready = gather_events(
            err, c, step["cross"][2], step["chain"][2], None,
            (max(times[0], done + 0.01),) + tuple(times[1:]), use_err
        )
        first, second, third = step["last_sums"]
        event(ready, sum_first, 1, c)
        event(ready + first, sum_second, 1, c)
        event(ready + first + 0.005, scatter_finish, c)
        event(ready + first + 0.005, gather_drain, err, c, step["cross"][2], step["chain"][2])
        event(ready + first + second, sum_third, 1, c)
        event(ready + first + second + third, close, c)
        closing = max(closing, ready)
    if flat:
        for b in range(n):
            event(last + 2.0 + b, turn, b)
            event(closing + 0.01 + (0.0 if b < n // 4 else first if b < 3 * n // 4 else first + second), finish_dec, b)
        event(closing - 1.0, turn_feat)
    for _, _, function in sorted(events, key=lambda e: e[:2]):
        function()
    for c in range(chunks):
        sum_finish(1, c)


def write_kernel(n, width, turned, gpre, gdec, gbenc, gbdec, genc_out, gdec_out, gbenc_out, gbdec_out, genc, sem):
    copies = [
        pltpu.make_async_copy(src, dst, sem.at[n + i])
        for i, (src, dst) in enumerate(
            ((gdec, gdec_out), (gbenc, gbenc_out), (gbdec, gbdec_out))
        )
    ]
    for copy in copies:
        copy.start()
    for b in range(n):
        lines = pl.ds(b * width, width)
        genc[lines, :] = dot(turned[lines, :], gpre[...]).astype(BF16)
        copies.append(pltpu.make_async_copy(genc.at[lines, :], genc_out.at[lines, :], sem.at[b]))
        copies[-1].start()
    for copy in copies:
        copy.wait()


def body(n, acts, w_enc, b_enc, w_dec, b_dec):
    local, enc, dec = acts[0], w_enc[0], w_dec[0]
    tokens, width = local.shape
    latents = enc.shape[1]
    depth = n // INNER
    flat = width % 128 == 0 and latents % 128 == 0
    unit = tokens // sum(SHARES)
    if flat and tokens % sum(SHARES) == 0 and unit % 32 == 0:
        sizes = [unit * s for s in SHARES]
    else:
        sizes = [tokens]
    chunks = len(sizes)
    plan = default_plan(depth, chunks)
    if PLAN is not None and chunks == len(SHARES) and depth == len(PLAN["chunks"][0]["line"]) + 1:
        plan = PLAN
    far = any(step["chain"][1] < depth - 1 for step in plan["chunks"])
    scale = tokens ** (-0.5)
    if not flat:
        dec = dec.reshape(latents, n, width).transpose(1, 0, 2)
    vmem = pl.BlockSpec(memory_space=pltpu.VMEM)
    hbm = pl.BlockSpec(memory_space=pl.ANY)
    dma = pltpu.SemaphoreType.DMA
    blocks = (n, tokens, width)
    hidden = (tokens, latents)
    side = pltpu.VMEM((depth, tokens, width), BF16)
    line = pltpu.VMEM((depth + 1, tokens, width), BF16)
    cross = pltpu.VMEM((tokens, width), BF16)
    kind = pltpu.VMEM if flat else jax.ShapeDtypeStruct
    small = (kind((1, latents), F32), kind((1, width), F32))
    inner = (blocks, blocks, hidden, hidden)
    if flat:
        outs = (
            pltpu.VMEM((n * width, tokens), BF16),
            pltpu.VMEM(hidden, BF16),
            pltpu.VMEM((latents, n * width), BF16),
        )
        extra = [pltpu.VMEM(shape, BF16) for shape in (blocks, blocks, hidden, (latents, tokens))]
    else:
        outs = tuple(jax.ShapeDtypeStruct(shape, BF16) for shape in inner)
        extra = []
    results = pl.pallas_call(
        functools.partial(step_kernel, n, sizes, plan, flat, scale),
        out_shape=outs + small,
        in_specs=[hbm] * 5,
        out_specs=(vmem,) * (len(outs) + 2),
        scratch_shapes=extra + [
            pltpu.VMEM(enc.shape, BF16),
            pltpu.VMEM(dec.shape, BF16),
            pltpu.VMEM((1, latents), F32),
            pltpu.VMEM((1, width), BF16),
            pltpu.VMEM((2,) + hidden, F32),
            pltpu.VMEM((depth, tokens, width), F32),
            side, side, line, line,
            cross, cross, cross, cross,
            pltpu.VMEM((2,) + hidden, BF16),
            pltpu.VMEM((2, 2, tokens // 2, latents), BF16),
            pltpu.VMEM((2,) + hidden, BF16),
            pltpu.VMEM(hidden, F32),
            side if far else pltpu.VMEM((1, 16, width), BF16),
            dma((5,)),
            dma((chunks, n)),
            dma((chunks, n)),
            dma((2, chunks, depth)),
            dma((chunks, depth)),
            dma((chunks, depth + 1)),
            dma((2, chunks, 2)),
            dma((chunks, depth)),
            dma((2, chunks, 4)),
        ],
        compiler_params=pltpu.CompilerParams(
            collective_id=0, has_side_effects=True,
            vmem_limit_bytes=VMEM_LIMIT - (4 * n * width * latents if flat else 0),
        ),
        name="step",
    )(local, enc, dec, b_enc[None, :], b_dec)
    gbenc, gbdec = results[-2:]
    if flat:
        held = [pltpu.with_memory_space_constraint(r, pltpu.VMEM) for r in results]
        genc, gdec, gbenc, gbdec = pl.pallas_call(
            functools.partial(write_kernel, n, width),
            out_shape=(
                jax.ShapeDtypeStruct((n * width, latents), BF16),
                jax.ShapeDtypeStruct((latents, n * width), BF16),
            ) + tuple(jax.ShapeDtypeStruct(r.shape, F32) for r in results[-2:]),
            in_specs=[vmem] * 5,
            out_specs=(hbm,) * 4,
            scratch_shapes=[pltpu.VMEM((n * width, latents), BF16), dma((n + 3,))],
            compiler_params=pltpu.CompilerParams(vmem_limit_bytes=8 * n * width * latents),
            name="write",
        )(*held)
    else:
        full, err, feat, gpre = results[:4]
        genc = jnp.einsum("btw,tl->bwl", full, gpre, preferred_element_type=F32)
        genc = genc.astype(BF16).reshape(n * width, latents)
        gdec = jnp.einsum("tl,btw->lbw", feat, err, preferred_element_type=F32)
        gdec = (scale * gdec).astype(BF16).reshape(latents, n * width)
    return genc[None], gdec[None], gbenc[0], gbdec


def solution(mesh):
    return jax.shard_map(
        functools.partial(body, mesh.shape["latent"]),
        mesh=mesh,
        in_specs=(
            P("layer", None, "latent"),
            P("layer", None, "latent"),
            P("latent"),
            P("layer", "latent", None),
            P("layer", "latent"),
        ),
        out_specs=(
            P("layer", None, "latent"),
            P("layer", "latent", None),
            P("latent"),
            P("layer", "latent"),
        ),
        check_vma=False,
    )
```

```python
import functools

import jax
import jax.numpy as jnp
from jax import lax
from jax.experimental import pallas as pl
from jax.experimental.pallas import tpu as pltpu
from jax.sharding import PartitionSpec as P

MESH = pl.DeviceIdType.MESH
F32 = jnp.float32
BF16 = jnp.bfloat16
INNER = 2
VMEM_LIMIT = 60 * 1024 * 1024
SHARES = (1, 1, 1, 1)
PLAN = {'use': 0.088,
 'chunks': [{'act': (1.653, [5.379, 17.95, 26.421], [20.826, 28.034, 28.439, 29.995]),
             'sums': (0.08, 10.405, 3.909),
             'out': 16.53,
             'line': [24.781, 53.549, 55.87],
             'near': 53.611,
             'own': 66.352,
             'done': 49.587,
             'err': (8.342, [73.948, 77.397, 89.794], [94.104, 89.88, 98.665, 109.267]),
             'last_sums': (10.487, 27.255, 56.675),
             'cross': (True, True, False),
             'chain': (3, 1, 3)},
            {'act': (0, [1.872, 6.068, 14.928], [13.569, 14.243, 18.59, 23.119]),
             'sums': (3.581, 3.316, 2.845),
             'out': 29.289,
             'line': [52.625, 44.425, 34.078],
             'near': 24.318,
             'own': 16.406,
             'done': 55.534,
             'err': (24.524, [66.338, 71.499, 85.811], [72.325, 95.07, 98.666, 103.516]),
             'last_sums': (6.426, 25.889, 71.057),
             'cross': (False, False, False),
             'chain': (3, 2, 3)},
            {'act': (1.53, [2.47, 9.524, 21.086], [16.35, 14.535, 27.595, 27.956]),
             'sums': (5.982, 10.669, 8.185),
             'out': 33.606,
             'line': [76.416, 67.271, 61.011],
             'near': 68.254,
             'own': 85.726,
             'done': 84.6,
             'err': (3.093, [100.283, 111.038, 98.974], [103.821, 124.235, 144.106, 127.222]),
             'last_sums': (37.069, 36.778, 50.644),
             'cross': (False, True, False),
             'chain': (3, 3, 2)},
            {'act': (8.103, [26.698, 30.062, 32.555], [25.325, 40.634, 37.702, 43.001]),
             'sums': (2.95, 7.984, 10.445),
             'out': 44.006,
             'line': [76.422, 72.264, 55.17],
             'near': 11.685,
             'own': 21.728,
             'done': 87.738,
             'err': (73.523, [107.214, 119.94, 123.367], [114.268, 171.21, 175.814, 183.56]),
             'last_sums': (28.002, 6.534, 64.422),
             'cross': (False, False, True),
             'chain': (3, 3, 2)}]}


def default_plan(depth, chunks):
    plan = []
    for c in range(chunks):
        begin, hop = 4.0 * c, 3.0
        act = begin, [begin + d * hop for d in range(1, depth)], [begin + (d + 1) * hop for d in range(depth)]
        out = begin + (depth + 3) * hop
        done = out + (depth + 1) * hop
        err = done, [done + d * hop for d in range(1, depth)], [done + (d + 1) * hop for d in range(depth)]
        plan.append(dict(
            act=act, sums=(hop / 2, hop, hop / 2), out=out, line=[out + (depth - d) * hop for d in range(1, depth)],
            near=out + 0.3, own=out + hop, done=done, err=err, last_sums=(hop / 2, hop, hop / 2),
            cross=(False, False, False), chain=(depth - 1,) * 3,
        ))
    return dict(use=0.3, chunks=plan)


def remote(src, dst, send, recv, axis, index):
    return pltpu.make_async_remote_copy(
        src_ref=src,
        dst_ref=dst,
        send_sem=send,
        recv_sem=recv,
        device_id={axis: index},
        device_id_type=MESH,
    )


def dot(a, b, dims=((1,), (0,))):
    return lax.dot_general(a, b, (dims, ((), ())), preferred_element_type=F32)


def step_kernel(n, sizes, plan, flat, scale, acts_hbm, enc_hbm, dec_hbm, benc_hbm, bdec_hbm, *refs):
    if flat:
        (turned, gpre, gdec, gbenc, gbdec), refs = refs[:5], refs[5:]
        (full, err, feat, feat_turned), refs = refs[:4], refs[4:]
    else:
        (full, err, feat, gpre, gbenc, gbdec), refs = refs[:6], refs[6:]
    (
        enc, dec, benc_ref, bdec_ref, part, own,
        side_out, side_in, line_out, line_in,
        xup_out, xup_in, xdown_out, xdown_in, sum_out, sum_in, total, gate,
        far_in, load_sem, block_send, block_recv, side_sem, line_send, line_recv, cross_sem, far_recv, sum_sem,
    ) = refs
    depth = n // INNER
    tokens, width = acts_hbm.shape
    chunks = len(sizes)
    me = lax.axis_index("latent")
    z, y = me // INNER, lax.rem(me, INNER)
    partner = z * INNER + 1 - y
    layer = lax.axis_index("layer")
    core = lax.rem(layer, 2)
    twin, opposite = layer + 1 - 2 * core, lax.rem(layer + 2, 4)
    not_top, not_bottom = z < depth - 1, z > 0

    barrier = pltpu.get_barrier_semaphore()

    def greet(axis, index):
        pl.semaphore_signal(barrier, inc=1, device_id={axis: index}, device_id_type=MESH)

    greet("latent", partner)
    pl.when(not_top)(lambda: greet("latent", me + INNER))
    pl.when(not_bottom)(lambda: greet("latent", me - INNER))
    greet("layer", twin)
    greet("layer", opposite)
    loads = [
        pltpu.make_async_copy(acts_hbm, full.at[me], load_sem.at[0]),
        pltpu.make_async_copy(benc_hbm, benc_ref, load_sem.at[1]),
        pltpu.make_async_copy(bdec_hbm, bdec_ref, load_sem.at[2]),
        pltpu.make_async_copy(enc_hbm, enc, load_sem.at[3]),
        pltpu.make_async_copy(dec_hbm, dec, load_sem.at[4]),
    ]
    for load in loads:
        load.start()
    pl.semaphore_wait(
        barrier, 3 + jnp.where(not_top, 1, 0) + jnp.where(not_bottom, 1, 0)
    )

    gbdec[...] = jnp.zeros_like(gbdec)
    gbenc[...] = jnp.zeros_like(gbenc)

    starts = [sum(sizes[:c]) for c in range(chunks)]

    def span(c):
        return pl.ds(starts[c], sizes[c])

    steps = plan["chunks"]

    def half(c, k):
        size = sizes[c] // 2
        return pl.ds(pl.multiple_of(starts[c] + k * size, size), size)

    def slot(c):
        return pl.ds(starts[c] // 2, sizes[c] // 2)

    def enc_rows(b):
        return enc[pl.ds(pl.multiple_of(b * width, width), width), :]

    def dec_columns(b):
        if flat:
            return dec[:, pl.ds(pl.multiple_of(b * width, width), width)]
        return dec[b]

    targets = (partner, me + INNER, me - INNER)

    def at_distance(d, up, use):
        at = z + d if up else z - d
        pl.when(at < depth if up else at >= 0)(lambda: use(at))

    def gather_copy(buf, c, b, way, source=None):
        spot = buf.at[b, span(c), :]
        return remote(
            spot if source is None else source, spot,
            block_send.at[c, b], block_recv.at[c, b], "latent", targets[way],
        )

    def gather_far(buf, c, at, source):
        spot = buf.at[me, span(c), :]
        return remote(
            spot if source is None else source, spot,
            block_send.at[c, me], block_recv.at[c, me], "latent", at * INNER + y,
        )

    def drain(buf, c, b, count, most):
        for k in range(1, most + 1):

            @pl.when(count == k)
            def _():
                spot = buf.at[pl.ds(0, k), span(c), :]
                remote(
                    spot, spot, block_send.at[c, b], block_recv.at[c, b], "latent", partner
                ).wait_send()

    def gather_own(buf, c, chain, source):
        for d in range(depth - 1, chain, -1):
            for up in (True, False):
                at_distance(d, up, lambda at: gather_far(buf, c, at, source).start())
        pl.when(not_top)(lambda: gather_copy(buf, c, me, 1, source).start())
        pl.when(not_bottom)(lambda: gather_copy(buf, c, me, 2, source).start())
        gather_copy(buf, c, me, 0, source).start()

    def gather_line(buf, c, cross, chain, d, below):
        def go(at):
            b = at * INNER + y
            gather_copy(buf, c, b, 0).wait_recv()
            if d < chain:
                way = 1 if below else 2
                pl.when(not_top if below else not_bottom)(lambda: gather_copy(buf, c, b, way).start())
            if not (cross and d == 1):
                gather_copy(buf, c, b, 0).start()

        at_distance(d, not below, go)

    def gather_side(buf, c, cross, d, below):
        def go(at):
            b = at * INNER + 1 - y
            gather_copy(buf, c, b, 0).wait_recv()
            if cross and d == 0:
                pl.when(not_top)(lambda: gather_copy(buf, c, b, 1).start())
                pl.when(not_bottom)(lambda: gather_copy(buf, c, b, 2).start())

        at_distance(d, not below, go)

    def one(condition):
        return jnp.where(condition, 1, 0)

    def gather_drain(buf, c, cross, chain):
        ends = one(not_top) + one(not_bottom)
        count = 1 + ends
        for d in range(chain + 1, depth):
            count = count + one(z + d < depth) + one(z >= d)
        drain(buf, c, me, count, depth + 1)
        for d in range(1, depth):
            for below in (True, False):

                def go(at):
                    count = 0 if cross and d == 1 else 1
                    if d < chain:
                        count = count + one(not_top if below else not_bottom)
                    drain(buf, c, at * INNER + y, count, 2)

                if d < chain or not (cross and d == 1):
                    at_distance(d, not below, go)
        if cross:
            drain(buf, c, partner, ends, 2)

    def on_block(d, below, side, use):
        at = z - d if below else z + d

        @pl.when(at >= 0 if below else at < depth)
        def _():
            use(at * INNER + (1 - y if side else y))

    events = []

    def event(time, function, *args):
        events.append((time, len(events), functools.partial(function, *args)))

    def gather_events(buf, c, cross, chain, source, times, use):
        begin, along, aside = times
        late = plan["use"]
        event(begin, gather_own, buf, c, chain, source)
        event(begin + 0.1, use, c, me)
        last = begin + 0.1
        for d in range(1, depth):
            at = max(along[d - 1], begin + 0.2)
            last = max(last, at + late)
            for below in (True, False):
                event(at, gather_line, buf, c, cross, chain, d, below)
                event(at + late, on_block, d, below, False, functools.partial(use, c))
        for d in range(depth):
            at = max(aside[d], begin + 0.2)
            last = max(last, at + late)
            for below in (True, False) if d else (True,):
                event(at, gather_side, buf, c, cross, d, below)
                event(at + late, on_block, d, below, True, functools.partial(use, c))
        return last + 0.05

    def sum_copy(s, c, phase):
        if phase == 0:
            src, dst = sum_out.at[s, half(c, 1 - core), :], sum_in.at[s, 0, slot(c), :]
        elif phase == 1:
            src, dst = sum_out.at[s, half(c, core), :], sum_in.at[s, 1, slot(c), :]
        else:
            src = dst = total.at[s, half(c, core), :]
        mark = 3 if phase == 1 and s else phase
        return remote(
            src, dst, sum_sem.at[0, c, mark], sum_sem.at[1, c, mark],
            "layer", opposite if phase == 1 else twin,
        )

    def sum_first(s, c):
        sum_out[s, half(c, 1 - core), :] = part[s, half(c, 1 - core), :].astype(BF16)
        sum_copy(s, c, 0).start()

    def sum_second(s, c):
        sum_copy(s, c, 0).wait_recv()
        value = part[s, half(c, core), :] + sum_in[s, 0, slot(c), :].astype(F32)
        sum_out[s, half(c, core), :] = value.astype(BF16)
        sum_copy(s, c, 1).start()

    def sum_third(s, c):
        sum_copy(s, c, 1).wait_recv()
        value = sum_out[s, half(c, core), :].astype(F32) + sum_in[s, 1, slot(c), :].astype(F32)
        total[s, half(c, core), :] = value.astype(BF16)
        sum_copy(s, c, 2).start()

    def sum_fourth(s, c):
        sum_copy(s, c, 2).wait_recv()

    def sum_finish(s, c):
        for phase in range(3):
            sum_copy(s, c, phase).wait_send()

    def use_act(c, b):
        value = dot(full[b, span(c), :], enc_rows(b))
        part[0, span(c), :] = value if b is me else part[0, span(c), :] + value

    def use_err(c, b):
        value = dot(err[b, span(c), :], dec_columns(b), ((1,), (1,)))
        part[1, span(c), :] = value if b is me else part[1, span(c), :] + value

    def activate(c):
        sum_fourth(0, c)
        wide = 4.0 * (total[0, span(c), :].astype(F32) + benc_ref[...])
        soft = jnp.maximum(wide, 0.0) + jnp.log1p(jnp.exp(-jnp.abs(wide)))
        feat[span(c), :] = (soft * 0.25).astype(BF16)

    def open_gate(c):
        wide = 4.0 * (total[0, span(c), :].astype(F32) + benc_ref[...])
        gate[span(c), :] = scale * jax.nn.sigmoid(wide)

    def term(c, b):
        return dot(feat[span(c), :], dec_columns(b))

    def side_copy(c, at):
        return remote(
            side_out.at[at, span(c), :], side_in.at[at, span(c), :],
            side_sem.at[0, c, at], side_sem.at[1, c, at], "latent", partner,
        )

    def land(at, up):
        return at + 1 if up else at

    def line_copy(c, at, up):
        return remote(
            line_out.at[at, span(c), :], line_in.at[land(at, up), span(c), :],
            line_send.at[c, at], line_recv.at[c, land(at, up)],
            "latent", me + INNER if up else me - INNER,
        )

    def far_copy(c, at, source):
        return remote(
            line_out.at[at, span(c), :], far_in.at[source, span(c), :],
            line_send.at[c, at], far_recv.at[c, source], "latent", at * INNER + y,
        )

    def cross_copy(c, up):
        out, spot = (xup_out, xup_in) if up else (xdown_out, xdown_in)
        k = 0 if up else 1
        return remote(
            out.at[span(c), :], spot.at[span(c), :], cross_sem.at[0, c, k], cross_sem.at[1, c, k],
            "latent", me + INNER if up else me - INNER,
        )

    def scatter_other(c, d, up):
        def go(at):
            value = term(c, at * INNER + 1 - y).astype(BF16)
            if steps[c]["cross"][1] and d == 1:
                out = xup_out if up else xdown_out
                out[span(c), :] = value
                cross_copy(c, up).start()
            else:
                side_out[at, span(c), :] = value
                side_copy(c, at).start()

        at_distance(d, up, go)

    def scatter_other_near(c):
        value = term(c, z * INNER + 1 - y)
        if not steps[c]["cross"][1]:
            side_out[z, span(c), :] = value.astype(BF16)
            side_copy(c, z).start()
            return
        own[z, span(c), :] = value
        for up, valid in ((True, not_bottom), (False, not_top)):

            @pl.when(valid)
            def _():
                cross_copy(c, up).wait_recv()
                own[z, span(c), :] = own[z, span(c), :] + (xup_in if up else xdown_in)[span(c), :].astype(F32)

        side_out[z, span(c), :] = own[z, span(c), :].astype(BF16)
        side_copy(c, z).start()

    def scatter_own(c, d, up):
        def go(at):
            own[at, span(c), :] = term(c, at * INNER + y)

        at_distance(d, up, go)

    def scatter_line(c, d, up):
        inner = not_bottom if up else not_top

        def go(at):
            value = own[at, span(c), :]
            if not (steps[c]["cross"][1] and d == 1):
                side_copy(c, at).wait_recv()
                value = value + side_in[at, span(c), :].astype(F32)

            chain = steps[c]["chain"][1]
            if d >= chain:
                line_out[at, span(c), :] = value.astype(BF16)
                (line_copy(c, at, up) if d == chain else far_copy(c, at, z)).start()
                return

            @pl.when(inner)
            def _():
                line_copy(c, at, up).wait_recv()
                line_out[at, span(c), :] = (
                    value + line_in[land(at, up), span(c), :].astype(F32)
                ).astype(BF16)

            @pl.when(jnp.logical_not(inner))
            def _():
                line_out[at, span(c), :] = value.astype(BF16)

            line_copy(c, at, up).start()

        at_distance(d, up, go)

    def scatter_last(c):
        side_copy(c, z).wait_recv()
        value = own[z, span(c), :] + side_in[z, span(c), :].astype(F32)
        own[z, span(c), :] = value + bdec_ref[...].astype(F32) - full[me, span(c), :].astype(F32)
        for up, valid in ((True, not_bottom), (False, not_top)):

            @pl.when(valid)
            def _():
                line_copy(c, z, up).wait_recv()
                own[z, span(c), :] = own[z, span(c), :] + line_in[land(z, up), span(c), :].astype(F32)

        for d in range(steps[c]["chain"][1] + 1, depth):
            for up in (True, False):

                def add(at):
                    far_copy(c, z, at).wait_recv()
                    own[z, span(c), :] = own[z, span(c), :] + far_in[at, span(c), :].astype(F32)

                at_distance(d, up, add)
        value = own[z, span(c), :].astype(BF16)
        err[me, span(c), :] = value
        gbdec[...] = gbdec[...] + scale * jnp.sum(value.astype(F32), axis=0, keepdims=True)

    def scatter_finish(c):
        for d in range(depth - 1, 0, -1):
            for up in (True, False):
                if steps[c]["cross"][1] and d == 1:
                    at_distance(d, up, lambda at: cross_copy(c, up).wait_send())
                else:
                    at_distance(d, up, lambda at: side_copy(c, at).wait_send())
                if d > steps[c]["chain"][1]:
                    at_distance(d, up, lambda at: far_copy(c, at, z).wait_send())
                else:
                    at_distance(d, up, lambda at: line_copy(c, at, up).wait_send())
        side_copy(c, z).wait_send()

    def close(c):
        sum_fourth(1, c)
        value = total[1, span(c), :].astype(F32) * gate[span(c), :]
        gbenc[...] = gbenc[...] + jnp.sum(value, axis=0, keepdims=True)
        gpre[span(c), :] = value.astype(BF16)

    def own_near(c):
        own[z, span(c), :] = term(c, z * INNER + y)

    def turn(b):
        turned[pl.ds(b * width, width), :] = full[b].T

    def turn_feat():
        feat_turned[...] = feat[...].T

    def finish_dec(b):
        columns = pl.ds(b * width, width)
        gdec[:, columns] = (scale * dot(feat_turned[...], err[b])).astype(BF16)

    source = lambda c: None
    event(-1.0, loads[0].wait)
    event(0.06, loads[3].wait)
    event(2.0, loads[1].wait)
    event(2.0, loads[2].wait)
    event(2.0, loads[4].wait)
    last = closing = 0.0
    for c in range(chunks):
        step = steps[c]
        ready = gather_events(
            full, c, step["cross"][0], step["chain"][0], source(c), step["act"], use_act

        )
        last = max(last, ready)
        first, second, third = step["sums"]
        event(ready, sum_first, 0, c)
        event(ready + first, sum_second, 0, c)
        event(ready + first + second, sum_third, 0, c)
        ready = ready + first + second + third
        event(ready, activate, c)
        begin = max(ready + 0.05, step["out"])
        for d in range(depth - 1, 0, -1):
            for up in (True, False):
                event(begin, scatter_other, c, d, up)
        for d in range(depth - 1, 0, -1):
            for up in (True, False):
                event(begin + 0.2, scatter_own, c, d, up)
                event(max(step["line"][d - 1], begin + 0.3), scatter_line, c, d, up)
        near = max(step["near"], begin + 0.1)
        event(near, scatter_other_near, c)
        mine = max(step["own"], near + 0.01)
        event(mine, own_near, c)
        event(mine, open_gate, c)
        event(mine, gather_drain, full, c, step["cross"][0], step["chain"][0])
        event(mine, sum_finish, 0, c)
        done = max(step["done"], mine + 0.01)
        event(done, scatter_last, c)
        times = step["err"]
        ready = gather_events(
            err, c, step["cross"][2], step["chain"][2], None,
            (max(times[0], done + 0.01),) + tuple(times[1:]), use_err
        )
        first, second, third = step["last_sums"]
        event(ready, sum_first, 1, c)
        event(ready + first, sum_second, 1, c)
        event(ready + first + 0.005, scatter_finish, c)
        event(ready + first + 0.005, gather_drain, err, c, step["cross"][2], step["chain"][2])
        event(ready + first + second, sum_third, 1, c)
        event(ready + first + second + third, close, c)
        closing = max(closing, ready)
    if flat:
        for b in range(n):
            event(last + 2.0 + b, turn, b)
            event(closing + 0.01 + (0.0 if b < n // 4 else first if b < 3 * n // 4 else first + second), finish_dec, b)
        event(closing - 1.0, turn_feat)
    for _, _, function in sorted(events, key=lambda e: e[:2]):
        function()
    for c in range(chunks):
        sum_finish(1, c)


def write_kernel(n, width, turned, gpre, gdec, gbenc, gbdec, genc_out, gdec_out, gbenc_out, gbdec_out, genc, sem):
    copies = [
        pltpu.make_async_copy(src, dst, sem.at[n + i])
        for i, (src, dst) in enumerate(
            ((gdec, gdec_out), (gbenc, gbenc_out), (gbdec, gbdec_out))
        )
    ]
    for copy in copies:
        copy.start()
    for b in range(n):
        lines = pl.ds(b * width, width)
        genc[lines, :] = dot(turned[lines, :], gpre[...]).astype(BF16)
        copies.append(pltpu.make_async_copy(genc.at[lines, :], genc_out.at[lines, :], sem.at[b]))
        copies[-1].start()
    for copy in copies:
        copy.wait()


def body(n, acts, w_enc, b_enc, w_dec, b_dec):
    local, enc, dec = acts[0], w_enc[0], w_dec[0]
    tokens, width = local.shape
    latents = enc.shape[1]
    depth = n // INNER
    flat = width % 128 == 0 and latents % 128 == 0
    unit = tokens // sum(SHARES)
    if flat and tokens % sum(SHARES) == 0 and unit % 32 == 0:
        sizes = [unit * s for s in SHARES]
    else:
        sizes = [tokens]
    chunks = len(sizes)
    plan = default_plan(depth, chunks)
    if PLAN is not None and chunks == len(SHARES) and depth == len(PLAN["chunks"][0]["line"]) + 1:
        plan = PLAN
    far = any(step["chain"][1] < depth - 1 for step in plan["chunks"])
    scale = tokens ** (-0.5)
    if not flat:
        dec = dec.reshape(latents, n, width).transpose(1, 0, 2)
    vmem = pl.BlockSpec(memory_space=pltpu.VMEM)
    hbm = pl.BlockSpec(memory_space=pl.ANY)
    dma = pltpu.SemaphoreType.DMA
    blocks = (n, tokens, width)
    hidden = (tokens, latents)
    side = pltpu.VMEM((depth, tokens, width), BF16)
    line = pltpu.VMEM((depth + 1, tokens, width), BF16)
    cross = pltpu.VMEM((tokens, width), BF16)
    kind = pltpu.VMEM if flat else jax.ShapeDtypeStruct
    small = (kind((1, latents), F32), kind((1, width), F32))
    inner = (blocks, blocks, hidden, hidden)
    if flat:
        outs = (
            pltpu.VMEM((n * width, tokens), BF16),
            pltpu.VMEM(hidden, BF16),
            pltpu.VMEM((latents, n * width), BF16),
        )
        extra = [pltpu.VMEM(shape, BF16) for shape in (blocks, blocks, hidden, (latents, tokens))]
    else:
        outs = tuple(jax.ShapeDtypeStruct(shape, BF16) for shape in inner)
        extra = []
    results = pl.pallas_call(
        functools.partial(step_kernel, n, sizes, plan, flat, scale),
        out_shape=outs + small,
        in_specs=[hbm] * 5,
        out_specs=(vmem,) * (len(outs) + 2),
        scratch_shapes=extra + [
            pltpu.VMEM(enc.shape, BF16),
            pltpu.VMEM(dec.shape, BF16),
            pltpu.VMEM((1, latents), F32),
            pltpu.VMEM((1, width), BF16),
            pltpu.VMEM((2,) + hidden, F32),
            pltpu.VMEM((depth, tokens, width), F32),
            side, side, line, line,
            cross, cross, cross, cross,
            pltpu.VMEM((2,) + hidden, BF16),
            pltpu.VMEM((2, 2, tokens // 2, latents), BF16),
            pltpu.VMEM((2,) + hidden, BF16),
            pltpu.VMEM(hidden, F32),
            side if far else pltpu.VMEM((1, 16, width), BF16),
            dma((5,)),
            dma((chunks, n)),
            dma((chunks, n)),
            dma((2, chunks, depth)),
            dma((chunks, depth)),
            dma((chunks, depth + 1)),
            dma((2, chunks, 2)),
            dma((chunks, depth)),
            dma((2, chunks, 4)),
        ],
        compiler_params=pltpu.CompilerParams(
            collective_id=0, has_side_effects=True,
            vmem_limit_bytes=VMEM_LIMIT - (4 * n * width * latents if flat else 0),
        ),
        name="step",
    )(local, enc, dec, b_enc[None, :], b_dec)
    gbenc, gbdec = results[-2:]
    if flat:
        held = [pltpu.with_memory_space_constraint(r, pltpu.VMEM) for r in results]
        genc, gdec, gbenc, gbdec = pl.pallas_call(
            functools.partial(write_kernel, n, width),
            out_shape=(
                jax.ShapeDtypeStruct((n * width, latents), BF16),
                jax.ShapeDtypeStruct((latents, n * width), BF16),
            ) + tuple(jax.ShapeDtypeStruct(r.shape, F32) for r in results[-2:]),
            in_specs=[vmem] * 5,
            out_specs=(hbm,) * 4,
            scratch_shapes=[pltpu.VMEM((n * width, latents), BF16), dma((n + 3,))],
            compiler_params=pltpu.CompilerParams(vmem_limit_bytes=8 * n * width * latents),
            name="write",
        )(*held)
    else:
        full, err, feat, gpre = results[:4]
        genc = jnp.einsum("btw,tl->bwl", full, gpre, preferred_element_type=F32)
        genc = genc.astype(BF16).reshape(n * width, latents)
        gdec = jnp.einsum("tl,btw->lbw", feat, err, preferred_element_type=F32)
        gdec = (scale * gdec).astype(BF16).reshape(latents, n * width)
    return genc[None], gdec[None], gbenc[0], gbdec


def solution(mesh):
    return jax.shard_map(
        functools.partial(body, mesh.shape["latent"]),
        mesh=mesh,
        in_specs=(
            P("layer", None, "latent"),
            P("layer", None, "latent"),
            P("latent"),
            P("layer", "latent", None),
            P("layer", "latent"),
        ),
        out_specs=(
            P("layer", None, "latent"),
            P("layer", "latent", None),
            P("latent"),
            P("layer", "latent"),
        ),
        check_vma=False,
    )
```
